128 devices in a mesh: gx: 8 (over y, core), gy: 16 (over z, x).
Axes of the slice: x: 4, y: 4, z: 4, core: 2. Of those that a mesh axis runs over, the one named last changes fastest.
Arguments:
- right_side: float32 [256, 512, 256], P('gx', 'gy'), may hold values from -32 to 32
- phase: int32 [256, 512, 256], P('gx', 'gy'), may hold values from 1 to 3
- table: float32 [4], replicated, may hold values from 0.3 to 3
Outputs:
- solution_field: float32 [256, 512, 256], P('gx', 'gy')
- residual: float32 [256, 512, 256], P('gx', 'gy')
- pre_residual: float32 [256, 512, 256], P('gx', 'gy')
- residual_image: float32 [256, 512, 256], P('gx', 'gy')
The draws below stay inside these ranges and needn't reach their ends.
Inputs may be any that keep to these rules, and one draw needn't show every extreme that they name: `phase`: labels 1 slag, 2 steel, 3 argon plume; label 0 stands for the lining outside the grid.
All inputs are finite; a program needn't handle non-finite values.
Results may differ from the reference program's by a relative error of at most 0.0003.
Values sent between devices are 32-bit elements; how exact they have to be, the bound alone decides.
No kernel may reach another device: no remote copies, remote signals or barrier semaphores. Data moves between devices by JAX's collectives and lax.ppermute only.
A program may use at most 64 MiB of HBM per device.

```python
import math
import jax
import jax.numpy as jnp

ITERS = 2
NCOND = 4
NX = 256
NY = 512
NZ = 256


def draw_right_side(key, part):
    first_key = jax.random.fold_in(key, 11)
    along_x = (jnp.arange(NX, dtype=jnp.float32) + 0.5) / NX
    along_y = (jnp.arange(NY, dtype=jnp.float32) + 0.5) / NY
    ramp = jnp.exp(1.1 * (along_x[:, None, None] + along_y[None, :, None]) - 1.1)
    base = jnp.clip(jax.random.normal(first_key, (NX, NY, NZ), jnp.float32), -6.0, 6.0)
    return (2.0 * ramp * base).astype(jnp.float32)


def set_ends(drawn, key, least, high):
    longest = drawn.shape.index(max(drawn.shape))
    spots = []
    for shift in (0, 1):
        where = [jax.random.randint(jax.random.fold_in(key, axis), (), 0, length) for axis, length in enumerate(drawn.shape)]
        where[longest] = (where[longest] + shift) % drawn.shape[longest]
        spots.append(tuple(where))
    return drawn.at[spots[0]].set(least).at[spots[1]].set(high)


def setup_inputs(seed: int = 0) -> dict:
    key_list = jax.random.split(jax.random.key(seed), 4)
    return {
        "right_side": draw_right_side(jax.random.fold_in(key_list[3], 71), 0),
        "phase": set_ends(jax.random.randint(key_list[1], (NX, NY, NZ), 1, 4), jax.random.fold_in(key_list[1], 1), 1, 3).astype(jnp.int32),
        "table": jnp.clip(jnp.exp(jax.random.uniform(key_list[2], (NCOND,), jnp.float32, math.log(0.3), math.log(3.0))), 0.3, 3.0),
    }


centre_value = 1.1
half_width = 0.9
ratio_sigma = centre_value / half_width
rho_first = 1.0 / ratio_sigma
rho_second = 1.0 / (2.0 * ratio_sigma - rho_first)
rho_third = 1.0 / (2.0 * ratio_sigma - rho_second)
start_scale = 1.0 / centre_value
keep_first = rho_second * rho_first
push_first = 2.0 * rho_second / half_width
keep_second = rho_third * rho_second
push_second = 2.0 * rho_third / half_width


def harmonic(left, right):
    return 2.0 * left * right / (left + right)


def coupling_set(sigma_padded):
    centre = sigma_padded[1:-1, 1:-1, 1:-1]
    to_west = harmonic(centre, sigma_padded[:-2, 1:-1, 1:-1])
    to_east = harmonic(centre, sigma_padded[2:, 1:-1, 1:-1])
    to_south = harmonic(centre, sigma_padded[1:-1, :-2, 1:-1])
    to_north = harmonic(centre, sigma_padded[1:-1, 2:, 1:-1])
    to_down = harmonic(centre, sigma_padded[1:-1, 1:-1, :-2])
    to_up = harmonic(centre, sigma_padded[1:-1, 1:-1, 2:])
    diagonal = to_west + to_east + to_south + to_north + to_down + to_up
    return (to_west, to_east, to_south, to_north, to_down, to_up, diagonal)


def padded_sigma(phase, table):
    return table[jnp.pad(phase, 1)]


def operate(field, phase, table):
    to_west, to_east, to_south, to_north, to_down, to_up, diagonal = coupling_set(padded_sigma(phase, table))
    padded = jnp.pad(field, 1)
    beside = (to_west * padded[:-2, 1:-1, 1:-1] + to_east * padded[2:, 1:-1, 1:-1]
              + to_south * padded[1:-1, :-2, 1:-1] + to_north * padded[1:-1, 2:, 1:-1]
              + to_down * padded[1:-1, 1:-1, :-2] + to_up * padded[1:-1, 1:-1, 2:])
    return diagonal * field - beside


def precondition(vector, phase, table):
    diagonal = coupling_set(padded_sigma(phase, table))[6]
    first = start_scale * (vector / diagonal)
    change = keep_first * first + push_first * ((vector - operate(first, phase, table)) / diagonal)
    second = first + change
    change = keep_second * change + push_second * ((vector - operate(second, phase, table)) / diagonal)
    return second + change


def reference(right_side, phase, table):
    solution_field = jnp.zeros_like(right_side)
    residual = right_side
    pre_residual = precondition(residual, phase, table)
    residual_image = operate(pre_residual, phase, table)
    image_dir = jnp.zeros_like(right_side)
    pre_dir = jnp.zeros_like(right_side)
    resid_dir = jnp.zeros_like(right_side)
    direction = jnp.zeros_like(right_side)
    energy_prev = jnp.float32(1.0)
    step_prev = jnp.float32(1.0)
    for iteration in range(ITERS):
        energy_now = jnp.sum(residual * pre_residual)
        curvature = jnp.sum(residual_image * pre_residual)
        pre_image = precondition(residual_image, phase, table)
        double_image = operate(pre_image, phase, table)
        if iteration == 0:
            step_size = energy_now / curvature
            image_dir = double_image
            pre_dir = pre_image
            resid_dir = residual_image
            direction = pre_residual
        else:
            momentum = energy_now / energy_prev
            step_size = energy_now / (curvature - momentum * energy_now / step_prev)
            image_dir = double_image + momentum * image_dir
            pre_dir = pre_image + momentum * pre_dir
            resid_dir = residual_image + momentum * resid_dir
            direction = pre_residual + momentum * direction
        solution_field = solution_field + step_size * direction
        residual = residual - step_size * resid_dir
        pre_residual = pre_residual - step_size * pre_dir
        residual_image = residual_image - step_size * image_dir
        energy_prev = energy_now
        step_prev = step_size
    return (solution_field, residual, pre_residual, residual_image)
```

```python
import jax
import jax.numpy as jnp
from jax import lax
from jax.experimental import pallas as pl
from jax.experimental.pallas import tpu as pltpu
from jax.sharding import PartitionSpec as P

centre_value = 1.1
half_width = 0.9
ratio_sigma = centre_value / half_width
rho_first = 1.0 / ratio_sigma
rho_second = 1.0 / (2.0 * ratio_sigma - rho_first)
rho_third = 1.0 / (2.0 * ratio_sigma - rho_second)
start_scale = 1.0 / centre_value
keep_first = rho_second * rho_first
push_first = 2.0 * rho_second / half_width
keep_second = rho_third * rho_second
push_second = 2.0 * rho_third / half_width

ZT = (1.0 + keep_first - push_first) * start_scale + push_first
ZS = push_first * start_scale
UZ = 1.0 + keep_second - push_second
UT = push_second - keep_second * start_scale
US = push_second

NB = 32
HB = 9
HL = 10
OFF = 12
YE = 56
XE = NB + 2 * HL
NZ = 256
VM = pl.BlockSpec(memory_space=pltpu.VMEM)
SM = pl.BlockSpec(memory_space=pltpu.SMEM)
f32 = jnp.float32


def shape(*dims):
    return jax.ShapeDtypeStruct(dims, f32)


def params(**more):
    return pltpu.CompilerParams(vmem_limit_bytes=60 * 1024 * 1024, **more)


def pack_kernel(rhs, phase, up, down):
    for x in range(NB):
        up[HB * x:HB * x + HB, :] = rhs[x, NB - HB:NB, :]
        down[HB * x:HB * x + HB, :] = rhs[x, 0:HB, :]
        lo = NB * HB + HL * x
        up[lo:lo + HL, :] = phase[x, NB - HL:NB, :].astype(f32)
        down[lo:lo + HL, :] = phase[x, 0:HL, :].astype(f32)


def join_kernel(rhs, phase, low, high, field, label, up, down):
    zero = jnp.zeros((OFF, NZ), f32)
    for x in range(NB):
        field[x, 0:OFF, :] = zero
        field[x, YE - OFF:YE, :] = zero
        label[x, 0:OFF, :] = zero
        label[x, YE - OFF:YE, :] = zero
        field[x, OFF:OFF + NB, :] = rhs[x]
        label[x, OFF:OFF + NB, :] = phase[x].astype(f32)
        field[x, OFF - HB:OFF, :] = low[HB * x:HB * x + HB, :]
        field[x, OFF + NB:OFF + NB + HB, :] = high[HB * x:HB * x + HB, :]
        lo = NB * HB + HL * x
        label[x, OFF - HL:OFF, :] = low[lo:lo + HL, :]
        label[x, OFF + NB:OFF + NB + HL, :] = high[lo:lo + HL, :]
    up[0:HB] = field[NB - HB:NB]
    up[HB:HB + HL] = label[NB - HL:NB]
    down[0:HB] = field[0:HB]
    down[HB:HB + HL] = label[0:HL]


def spread(couplings, z_ref, x):
    west, east, south, north, below, above = couplings
    here = z_ref[x]
    return (
        (west[x] * z_ref[x - 1] + east[x] * z_ref[x + 1])
        + (south[x] * pltpu.roll(here, 1, 0) + north[x] * pltpu.roll(here, YE - 1, 0))
        + (below[x] * pltpu.roll(here, 1, 1) + above[x] * pltpu.roll(here, NZ - 1, 1))
    )


def composite(couplings, t_ref, z_ref, u_ref, next_ref, halo):
    def first(x, _):
        z_ref[x] = ZT * t_ref[x] + ZS * spread(couplings, t_ref, x)
        return 0

    def second(x, _):
        u_ref[x] = UZ * z_ref[x] + UT * t_ref[x] + US * spread(couplings, z_ref, x)
        return 0

    def third(x, _):
        next_ref[x] = (t_ref[x] - u_ref[x]) + spread(couplings, u_ref, x)
        return 0

    for step, rows in ((first, halo + 2), (second, halo + 1), (third, halo)):
        lax.fori_loop(HL - rows, HL + NB + rows, step, 0)


def main_kernel(table, field, label, low, high, west, east, south, north, below, above,
                t0, t1, t2, u0, u1, diag, sums, half, z_ref):
    lining = 0.5 / table[0]
    first_kind = 0.5 / table[1]
    second_kind = 0.5 / table[2]
    third_kind = 0.5 / table[3]

    def kind(labels):
        return jnp.where(labels == 1.0, first_kind, jnp.where(
            labels == 2.0, second_kind, jnp.where(labels == 3.0, third_kind, lining)))

    def fetch_own(x, _):
        half[x + HL] = label[x]
        t0[x + HL] = field[x]
        return 0

    def fetch_low(x, _):
        half[x] = low[x + HB]
        half[x + HL + NB] = high[x + HB]
        return 0

    def fetch_field(x, _):
        t0[x + 1] = low[x]
        t0[x + HL + NB] = high[x]
        return 0

    lax.fori_loop(0, NB, fetch_own, 0)
    lax.fori_loop(0, HL, fetch_low, 0)
    lax.fori_loop(0, HB, fetch_field, 0)

    lane = lax.broadcasted_iota(jnp.int32, (YE, NZ), 1)
    at_low = lane == 0
    at_high = lane == NZ - 1

    def couple(x, carry):
        to_west, here = carry
        labels = half[x]
        inside = labels > 0.0
        beyond = kind(half[x + 1])
        to_east = 1.0 / (here + beyond)
        to_north = 1.0 / (here + pltpu.roll(here, YE - 1, 0))
        to_south = pltpu.roll(to_north, 1, 0)
        to_up = 1.0 / (here + jnp.where(at_high, lining, pltpu.roll(here, NZ - 1, 1)))
        to_down = jnp.where(at_low, 1.0 / (here + lining), pltpu.roll(to_up, 1, 1))
        whole = to_west + to_east + to_south + to_north + to_down + to_up
        inverse = jnp.where(inside, 1.0 / whole, 0.0)
        west[x] = to_west * inverse
        east[x] = to_east * inverse
        south[x] = to_south * inverse
        north[x] = to_north * inverse
        below[x] = jnp.where(at_low, 0.0, to_down * inverse)
        above[x] = jnp.where(at_high, 0.0, to_up * inverse)
        t0[x] = t0[x] * inverse
        diag[x] = whole
        return to_east, beyond

    here = kind(half[1])
    lax.fori_loop(1, XE - 1, couple, (1.0 / (kind(half[0]) + here), here))

    couplings = (west, east, south, north, below, above)
    composite(couplings, t0, z_ref, u0, t1, 6)
    composite(couplings, t1, z_ref, u1, t2, 3)

    row = lax.broadcasted_iota(jnp.int32, (YE, NZ), 0)
    own = (row >= OFF) & (row < OFF + NB)

    def dots(x, carry):
        s0, s1, s2, s3 = carry
        du0 = jnp.where(own, diag[x] * u0[x], 0.0)
        du1 = jnp.where(own, diag[x] * u1[x], 0.0)
        return (s0 + t0[x] * du0, s1 + t1[x] * du0, s2 + t1[x] * du1, s3 + t2[x] * du1)

    zero = jnp.zeros((YE, NZ), f32)
    parts = lax.fori_loop(HL, HL + NB, dots, (zero, zero, zero, zero))
    place = lax.broadcasted_iota(jnp.int32, (8, 128), 1)
    line = jnp.zeros((8, 128), f32)
    for k, part in enumerate(parts):
        line = jnp.where(place == k, jnp.sum(part), line)
    sums[...] = line


def last_kernel(west, east, south, north, below, above, t2, u2, t3, z_ref, w_ref):
    composite((west, east, south, north, below, above), t2, z_ref, w_ref, t3, 0)

    def keep(x, _):
        u2[x] = w_ref[x]
        return 0

    lax.fori_loop(HL, HL + NB, keep, 0)


CHUNK = 4


def final_kernel(sums, t0, t1, t2, t3, u0, u1, u2, diag, solution_out, residual_out, pre_out,
                 image_out, bufs, sems):
    total = jnp.sum(sums[...], axis=0, keepdims=True)
    m0, m1, m2, m3 = (total[0:1, k:k + 1] for k in range(4))
    curvature = m0 - m1
    step_one = m0 / curvature
    off_one = -m1 / curvature
    energy = off_one * off_one * m0 + 2.0 * off_one * step_one * m1 + step_one * step_one * m2
    bend = (off_one * off_one * (m0 - m1) + 2.0 * off_one * step_one * (m1 - m2)
            + step_one * step_one * (m2 - m3))
    momentum = energy / m0
    step_two = energy / (bend - momentum * energy / step_one)
    c2 = step_one * step_two
    c1 = step_one + step_two * (1.0 + momentum) - 2.0 * c2
    c0 = off_one * (1.0 - step_two) - step_two * momentum
    s0 = c1 + c2
    outs = (solution_out, residual_out, pre_out, image_out)
    copies = []
    for chunk in range(NB // CHUNK):
        def body(k, _):
            x = chunk * CHUNK + k
            e = x + HL
            own = (e, slice(OFF, OFF + NB))
            v0, v1, v2, v3 = t0[e], t1[e], t2[e], t3[e]
            w0, w1, w2 = u0[e], u1[e], u2[e]
            d = diag[e]
            part = slice(OFF, OFF + NB)
            bufs[0, x] = (s0 * w0 + c2 * w1)[part]
            bufs[1, x] = (d * (c0 * v0 + c1 * v1 + c2 * v2))[part]
            bufs[2, x] = (c0 * w0 + c1 * w1 + c2 * w2)[part]
            bufs[3, x] = (d * (c0 * (v0 - v1) + c1 * (v1 - v2) + c2 * (v2 - v3)))[part]
            return 0
        lax.fori_loop(0, CHUNK, body, 0)
        rows = slice(chunk * CHUNK, (chunk + 1) * CHUNK)
        for k in range(4):
            copy = pltpu.make_async_copy(bufs.at[k, rows], outs[k].at[rows], sems.at[chunk, k])
            copy.start()
            copies.append(copy)
    for copy in copies:
        copy.wait()


def neighbours(axis):
    count = lax.axis_size(axis)
    forward = [(i, i + 1) for i in range(count - 1)]
    return forward, [(target, source) for source, target in forward]


def swap(up, down, axis):
    forward, backward = neighbours(axis)
    return lax.ppermute(up, axis, forward), lax.ppermute(down, axis, backward)


def local(right_side, phase, table):
    up, down = pl.pallas_call(
        pack_kernel, name="pack", in_specs=[VM] * 2, out_specs=[VM] * 2,
        out_shape=[shape(NB * (HB + HL), NZ)] * 2, compiler_params=params(),
    )(right_side, phase)
    low, high = swap(up, down, "gy")
    field, label, up, down = pl.pallas_call(
        join_kernel, name="join", in_specs=[VM] * 4, out_specs=[VM] * 4,
        out_shape=[shape(NB, YE, NZ)] * 2 + [shape(HB + HL, YE, NZ)] * 2,
        compiler_params=params(),
    )(right_side, phase, low, high)
    low, high = swap(up, down, "gx")
    ext = shape(XE, YE, NZ)
    scratch = pltpu.VMEM((XE, YE, NZ), f32)
    *couplings, t0, t1, t2, u0, u1, diag, sums = pl.pallas_call(
        main_kernel, name="main", in_specs=[SM] + [VM] * 4, out_specs=[VM] * 13,
        out_shape=[ext] * 12 + [shape(8, 128)],
        scratch_shapes=[scratch, scratch], compiler_params=params(),
    )(table, field, label, low, high)
    across = lax.all_to_all(sums, "gx", 0, 0, tiled=True)
    across = jnp.broadcast_to(jnp.sum(across, 0, keepdims=True), (16, 128))
    gathered = lax.all_to_all(across, "gy", 0, 0, tiled=True)
    u2, t3 = pl.pallas_call(
        last_kernel, name="last", in_specs=[VM] * 7, out_specs=[VM] * 2,
        out_shape=[ext] * 2, scratch_shapes=[scratch, scratch], compiler_params=params(),
        cost_estimate=pl.CostEstimate(flops=20000000, bytes_accessed=12000000, transcendentals=0),
    )(*couplings, t2)
    brick = shape(NB, NB, NZ)
    hbm = pl.BlockSpec(memory_space=pl.ANY)
    return pl.pallas_call(
        final_kernel, name="final", in_specs=[VM] * 9, out_specs=[hbm] * 4,
        out_shape=[brick] * 4,
        scratch_shapes=[pltpu.VMEM((4, NB, NB, NZ), f32),
                        pltpu.SemaphoreType.DMA((NB // CHUNK, 4))],
        compiler_params=params(),
    )(gathered, t0, t1, t2, t3, u0, u1, u2, diag)


def solution(mesh):
    placed = (P("gx", "gy", None), P("gx", "gy", None), P())
    return jax.shard_map(
        local,
        mesh=mesh,
        in_specs=placed,
        out_specs=(P("gx", "gy", None),) * 4,
        check_vma=False,
    )
```

```python
import jax
import jax.numpy as jnp
from jax import lax
from jax.experimental import pallas as pl
from jax.experimental.pallas import tpu as pltpu
from jax.sharding import PartitionSpec as P

centre_value = 1.1
half_width = 0.9
ratio_sigma = centre_value / half_width
rho_first = 1.0 / ratio_sigma
rho_second = 1.0 / (2.0 * ratio_sigma - rho_first)
rho_third = 1.0 / (2.0 * ratio_sigma - rho_second)
start_scale = 1.0 / centre_value
keep_first = rho_second * rho_first
push_first = 2.0 * rho_second / half_width
keep_second = rho_third * rho_second
push_second = 2.0 * rho_third / half_width

ZT = (1.0 + keep_first - push_first) * start_scale + push_first
ZS = push_first * start_scale
UZ = 1.0 + keep_second - push_second
UT = push_second - keep_second * start_scale
US = push_second

NB = 32
HB = 9
HL = 10
OFF = 12
YE = 56
XE = NB + 2 * HL
NZ = 256
VM = pl.BlockSpec(memory_space=pltpu.VMEM)
SM = pl.BlockSpec(memory_space=pltpu.SMEM)
f32 = jnp.float32


def shape(*dims):
    return jax.ShapeDtypeStruct(dims, f32)


def params(mib):
    return pltpu.CompilerParams(vmem_limit_bytes=mib * 1024 * 1024)

HALF = NZ // 2


def lanes(h):
    return slice(HALF * h, HALF * h + HALF)


def pack_kernel(rhs, phase, up, down):
    for x in range(NB):
        lo = NB * HB + HL * x
        for h in range(2):
            up[h, HB * x:HB * x + HB] = rhs[x, NB - HB:NB, lanes(h)]
            down[h, HB * x:HB * x + HB] = rhs[x, 0:HB, lanes(h)]
            up[h, lo:lo + HL] = phase[x, NB - HL:NB, lanes(h)].astype(f32)
            down[h, lo:lo + HL] = phase[x, 0:HL, lanes(h)].astype(f32)


def join_kernel(rhs, phase, low, high, field, label, up, down):
    edge = jnp.zeros((2, OFF - HL, HALF), f32)
    for x in range(NB):
        lo = NB * HB + HL * x
        for ref, width, base in ((field, HB, HB * x), (label, HL, lo)):
            own = rhs[x] if ref is field else phase[x].astype(f32)
            ref[x, :, 0:8] = jnp.zeros((2, 8, HALF), f32)
            ref[x, :, YE - 8:YE] = jnp.zeros((2, 8, HALF), f32)
            for h in range(2):
                ref[x, h, OFF:OFF + NB] = own[:, lanes(h)]
                ref[x, h, OFF - width:OFF] = low[h, base:base + width]
                ref[x, h, OFF + NB:OFF + NB + width] = high[h, base:base + width]
    up[0:HB] = field[NB - HB:NB]
    up[HB:HB + HL] = label[NB - HL:NB]
    down[0:HB] = field[0:HB]
    down[HB:HB + HL] = label[0:HL]


def machine(table, label_at, field_at, arrays):
    west, east, south, north, below, above, diag, t, z, u = arrays
    lining = 0.5 / table[0]
    first_kind = 0.5 / table[1]
    second_kind = 0.5 / table[2]
    third_kind = 0.5 / table[3]
    lane = lax.broadcasted_iota(jnp.int32, (YE, HALF), 1)
    at_low = lane == 0
    at_high = lane == HALF - 1
    real = slice(8, 8 + YE)

    def kind(labels):
        return jnp.where(labels == 1.0, first_kind, jnp.where(
            labels == 2.0, second_kind, jnp.where(labels == 3.0, third_kind, lining)))

    def clear(refs):
        def body(x, _):
            for ref in refs:
                ref[x, :, 0:8] = jnp.zeros((2, 8, HALF), f32)
                ref[x, :, 8 + YE:16 + YE] = jnp.zeros((2, 8, HALF), f32)
            return 0
        lax.fori_loop(0, XE, body, 0)

    def couple(start, stop):
        def body(x, carry):
            to_west, here = carry
            beyond = tuple(kind(label_at(x + 1, h)) for h in range(2))
            to_east = tuple(1.0 / (here[h] + beyond[h]) for h in range(2))
            to_north = tuple(1.0 / (here[h] + pltpu.roll(here[h], YE - 1, 0)) for h in range(2))
            after = tuple(pltpu.roll(here[h], HALF - 1, 1) for h in range(2))
            to_up = (1.0 / (here[0] + jnp.where(at_high, after[1], after[0])),
                     1.0 / (here[1] + jnp.where(at_high, lining, after[1])))
            moved = tuple(pltpu.roll(to_up[h], 1, 1) for h in range(2))
            to_down = (jnp.where(at_low, 1.0 / (here[0] + lining), moved[0]),
                       jnp.where(at_low, moved[0], moved[1]))
            for h in range(2):
                to_south = pltpu.roll(to_north[h], 1, 0)
                whole = (to_west[h] + to_east[h] + to_south + to_north[h] + to_down[h] + to_up[h])
                inverse = jnp.where(label_at(x, h) > 0.0, 1.0 / whole, 0.0)
                west[x, h] = to_west[h] * inverse
                east[x, h] = to_east[h] * inverse
                south[x, h] = to_south * inverse
                north[x, h] = to_north[h] * inverse
                down = to_down[h] * inverse
                rise = to_up[h] * inverse
                below[x, h] = jnp.where(at_low, 0.0, down) if h == 0 else down
                above[x, h] = jnp.where(at_high, 0.0, rise) if h == 1 else rise
                t[x, h, real] = field_at(x, h) * inverse
                diag[x, h] = whole
            return to_east, beyond

        here = tuple(kind(label_at(start, h)) for h in range(2))
        to_west = tuple(1.0 / (kind(label_at(start - 1, h)) + here[h]) for h in range(2))
        lax.fori_loop(start, stop, body, (to_west, here))

    def spread(ref, x, finish):
        here = tuple(ref[x, h, real] for h in range(2))
        back = tuple(pltpu.roll(here[h], 1, 1) for h in range(2))
        ahead = tuple(pltpu.roll(here[h], HALF - 1, 1) for h in range(2))
        lower = (back[0], jnp.where(at_low, back[0], back[1]))
        upper = (jnp.where(at_high, ahead[1], ahead[0]), ahead[1])
        for h in range(2):
            total = (
                (west[x, h] * ref[x - 1, h, real] + east[x, h] * ref[x + 1, h, real])
                + (south[x, h] * ref[x, h, 7:7 + YE] + north[x, h] * ref[x, h, 9:9 + YE])
                + (below[x, h] * lower[h] + above[x, h] * upper[h])
            )
            finish(h, here[h], total)

    def first(x, _):
        def finish(h, here, total):
            z[x, h, real] = ZT * here + ZS * total
        spread(t, x, finish)
        return 0

    def second(x, _):
        def finish(h, here, total):
            u[x, h, real] = UZ * here + UT * t[x, h, real] + US * total
        spread(z, x, finish)
        return 0

    def third(x, _):
        def finish(h, here, total):
            t[x, h, real] = (t[x, h, real] - here) + total
        spread(u, x, finish)
        return 0

    def run(stage, ranges):
        for start, stop in ranges:
            size = stop - start
            unroll = 4 if size % 4 == 0 else 3 if size % 3 == 0 else 2 if size % 2 == 0 else 1
            lax.fori_loop(start, stop, (first, second, third)[stage % 3], 0,
                          unroll=unroll if size > unroll else True)

    def run_sides(stage, low, high, size):
        step = (first, second, third)[stage % 3]

        def body(i, _):
            step(low + i, 0)
            step(high + i, 0)
            return 0
        lax.fori_loop(0, size, body, 0, unroll=2)

    def keep(ranges, u_out, r_out, pairs):
        own = slice(8 + OFF, 8 + OFF + NB)
        zero = jnp.zeros((NB, HALF), f32)

        def body(x, carry):
            totals = list(carry)
            for h in range(2):
                pre = u[x, h, own]
                res = t[x, h, own] * diag[x, h, OFF:OFF + NB]
                u_out[x - HL, :, lanes(h)] = pre
                r_out[x - HL, :, lanes(h)] = res
                for k, other in enumerate(pairs):
                    left = res if other is None else other[x - HL, :, lanes(h)]
                    totals[k] = totals[k] + left * pre
            return tuple(totals)

        totals = (zero,) * len(pairs)
        for start, stop in ranges:
            totals = lax.fori_loop(start, stop, body, totals)
        return totals

    return clear, couple, run, run_sides, keep


def as_line(parts):
    place = lax.broadcasted_iota(jnp.int32, (8, 128), 1)
    line = jnp.zeros((8, 128), f32)
    for k, part in enumerate(parts):
        line = jnp.where(place == k, jnp.sum(part), line)
    return line


LO, HI = HL, HL + NB
SUM_OF = ((None,), (None,), ())


def inner_kernel(table, rhs, field, label, *refs):
    arrays, kept, sums = refs[:10], refs[10:16], refs[16]
    r1, r2, r3, u0, u1, u2 = kept
    clear, couple, run, _, keep = machine(
        table, lambda x, h: label[x - HL, h], lambda x, h: field[x - HL, h], arrays)
    clear(arrays[7:])
    couple(LO + 1, HI - 1)
    parts = ()
    for stage in range(9):
        run(stage, ((LO + 2 + stage, HI - 2 - stage),))
        if stage == 2:
            parts += keep(((LO + 2 + stage, HI - 2 - stage),), u0, r1, (rhs, None))
        if stage == 5:
            parts += keep(((LO + 2 + stage, HI - 2 - stage),), u1, r2, (r1, None))
        if stage == 8:
            keep(((LO + 2 + stage, HI - 2 - stage),), u2, r3, ())
    sums[...] = as_line(parts)


def outer_kernel(table, rhs, field, label, low, high, part_sums, *refs):
    arrays, kept, sums, labels = refs[16:26], refs[26:32], refs[32], refs[33]
    r1, r2, r3, u0, u1, u2 = kept
    t = arrays[8]
    for x in range(HL):
        labels[0, x] = low[HB + x]
        labels[1, x + 2] = high[HB + x]
    for x in range(2):
        labels[0, HL + x] = label[x]
        labels[1, x] = label[NB - 2 + x]
    t[LO, :, 8:8 + YE] = field[0]
    t[HI - 1, :, 8:8 + YE] = field[NB - 1]
    for x in range(HB):
        t[LO - HB + x, :, 8:8 + YE] = low[x]
        t[HI + x, :, 8:8 + YE] = high[x]

    def field_at(x, h):
        return t[x, h, 8:8 + YE]

    for side, base, start in ((0, 0, 1), (1, HI - 2, HI - 1)):
        couple = machine(table, lambda x, h: labels[side, x - base, h], field_at, arrays)[1]
        couple(start, start + HL)
    _, _, _, run_sides, keep = machine(table, None, None, arrays)
    parts = ()
    for stage in range(9):
        run_sides(stage, 2 + stage, HI - 2 - stage, HL)
        rest = ((LO, LO + 2 + stage), (HI - 2 - stage, HI))
        if stage == 2:
            parts += keep(rest, u0, r1, (rhs, None))
        if stage == 5:
            parts += keep(rest, u1, r2, (r1, None))
        if stage == 8:
            keep(rest, u2, r3, ())
    sums[...] = part_sums[...] + as_line(parts)


INNER, OUTER = 2, 4
CHUNK = 4


def final_kernel(sums, r0, r1, r2, r3, u0, u1, u2, solution_out, residual_out, pre_out,
                 image_out, bufs, sems):
    total = jnp.sum(sums[...], axis=0, keepdims=True)
    m0, m1, m2, m3 = (total[0:1, k:k + 1] for k in range(4))
    curvature = m0 - m1
    step_one = m0 / curvature
    off_one = -m1 / curvature
    energy = off_one * off_one * m0 + 2.0 * off_one * step_one * m1 + step_one * step_one * m2
    bend = (off_one * off_one * (m0 - m1) + 2.0 * off_one * step_one * (m1 - m2)
            + step_one * step_one * (m2 - m3))
    momentum = energy / m0
    step_two = energy / (bend - momentum * energy / step_one)
    c2 = step_one * step_two
    c1 = step_one + step_two * (1.0 + momentum) - 2.0 * c2
    c0 = off_one * (1.0 - step_two) - step_two * momentum
    s0 = c1 + c2
    outs = (solution_out, residual_out, pre_out, image_out)
    copies = []
    for chunk in range(NB // CHUNK):
        def body(k, _):
            x = chunk * CHUNK + k
            v0, v1, v2, v3 = r0[x], r1[x], r2[x], r3[x]
            w0, w1, w2 = u0[x], u1[x], u2[x]
            bufs[0, x] = s0 * w0 + c2 * w1
            bufs[1, x] = c0 * v0 + c1 * v1 + c2 * v2
            bufs[2, x] = c0 * w0 + c1 * w1 + c2 * w2
            bufs[3, x] = c0 * (v0 - v1) + c1 * (v1 - v2) + c2 * (v2 - v3)
            return 0
        lax.fori_loop(0, CHUNK, body, 0)
        rows = slice(chunk * CHUNK, (chunk + 1) * CHUNK)
        for k in range(4):
            copy = pltpu.make_async_copy(bufs.at[k, rows], outs[k].at[rows], sems.at[chunk, k])
            copy.start()
            copies.append(copy)
    for copy in copies:
        copy.wait()


def neighbours(axis):
    count = lax.axis_size(axis)
    forward = [(i, i + 1) for i in range(count - 1)]
    return forward, [(target, source) for source, target in forward]


def swap(up, down, axis):
    forward, backward = neighbours(axis)
    return lax.ppermute(up, axis, forward), lax.ppermute(down, axis, backward)


def local(right_side, phase, table):
    up, down = pl.pallas_call(
        pack_kernel, name="pack", in_specs=[VM] * 2, out_specs=[VM] * 2,
        out_shape=[shape(2, NB * (HB + HL), HALF)] * 2, compiler_params=params(4),
    )(right_side, phase)
    low, high = swap(up, down, "gy")
    field, label, up, down = pl.pallas_call(
        join_kernel, name="join", in_specs=[VM] * 4, out_specs=[VM] * 4,
        out_shape=[shape(NB, 2, YE, HALF)] * 2 + [shape(HB + HL, 2, YE, HALF)] * 2,
        compiler_params=params(14),
    )(right_side, phase, low, high)
    low, high = swap(up, down, "gx")
    brick = shape(NB, NB, NZ)
    state = [shape(XE, 2, YE, HALF)] * 7 + [shape(XE, 2, YE + 16, HALF)] * 3 + [brick] * 6
    *kept, sums = pl.pallas_call(
        inner_kernel, name="inner", in_specs=[SM] + [VM] * 3, out_specs=[VM] * 17,
        out_shape=state + [shape(8, 128)], compiler_params=params(INNER),
        cost_estimate=pl.CostEstimate(flops=30000000, bytes_accessed=30000000, transcendentals=0),
    )(table, right_side, field, label)
    *kept, sums = pl.pallas_call(
        outer_kernel, name="outer", in_specs=[SM] + [VM] * 22, out_specs=[VM] * 17,
        out_shape=state + [shape(8, 128)], compiler_params=params(OUTER),
        scratch_shapes=[pltpu.VMEM((2, HL + 2, 2, YE, HALF), f32)],
        input_output_aliases={7 + k: k for k in range(16)},
    )(table, right_side, field, label, low, high, sums, *kept)
    kept = kept[10:]
    gathered = lax.all_to_all(
        jnp.broadcast_to(sums[0:1], (128, 128)), ("gx", "gy"), 0, 0, tiled=True)
    hbm = pl.BlockSpec(memory_space=pl.ANY)
    return pl.pallas_call(
        final_kernel, name="final", in_specs=[VM] * 8, out_specs=[hbm] * 4,
        out_shape=[brick] * 4,
        scratch_shapes=[pltpu.VMEM((4, NB, NB, NZ), f32),
                        pltpu.SemaphoreType.DMA((NB // CHUNK, 4))],
        compiler_params=params(14),
    )(gathered, right_side, *kept)


def solution(mesh):
    placed = (P("gx", "gy", None), P("gx", "gy", None), P())
    return jax.shard_map(
        local,
        mesh=mesh,
        in_specs=placed,
        out_specs=(P("gx", "gy", None),) * 4,
        check_vma=False,
    )
```

```python
import functools

import jax
import jax.numpy as jnp
from jax import lax
from jax.experimental import pallas as pl
from jax.experimental.pallas import tpu as pltpu
from jax.sharding import PartitionSpec as P

centre_value = 1.1
half_width = 0.9
ratio_sigma = centre_value / half_width
rho_first = 1.0 / ratio_sigma
rho_second = 1.0 / (2.0 * ratio_sigma - rho_first)
rho_third = 1.0 / (2.0 * ratio_sigma - rho_second)
start_scale = 1.0 / centre_value
keep_first = rho_second * rho_first
push_first = 2.0 * rho_second / half_width
keep_second = rho_third * rho_second
push_second = 2.0 * rho_third / half_width

ZT = (1.0 + keep_first - push_first) * start_scale + push_first
ZS = push_first * start_scale
UZ = 1.0 + keep_second - push_second
UT = push_second - keep_second * start_scale
US = push_second

NB = 32
HB = 9
HL = 10
OFF = 12
YE = 56
XE = NB + 2 * HL
NZ = 256
VM = pl.BlockSpec(memory_space=pltpu.VMEM)
SM = pl.BlockSpec(memory_space=pltpu.SMEM)
f32 = jnp.float32


def shape(*dims):
    return jax.ShapeDtypeStruct(dims, f32)


def params(mib):
    return pltpu.CompilerParams(vmem_limit_bytes=mib * 1024 * 1024)

HALF = NZ // 2
FULL, NEAR = (0, YE), (8, YE - 8)
NB_NEAR, NL_NEAR = 4, 5
SENT = (NB_NEAR + NL_NEAR) * YE + (HB - NB_NEAR + HL - NL_NEAR) * (YE - 16)


def rows_of(slab):
    return slice(slab[0], slab[1])


def held(slab):
    return slice(slab[0] + 8, slab[1] + 8)


def sent_rows(distance, label):
    near, far = (NL_NEAR, HL - NL_NEAR) if label else (NB_NEAR, HB - NB_NEAR)
    if distance <= near:
        start = (NB_NEAR * YE if label else 0) + (distance - 1) * YE
        return slice(start, start + YE), FULL
    base = (NB_NEAR + NL_NEAR) * YE + ((HB - NB_NEAR) * (YE - 16) if label else 0)
    start = base + (distance - near - 1) * (YE - 16)
    return slice(start, start + YE - 16), NEAR


def lanes(h):
    return slice(HALF * h, HALF * h + HALF)


def pack_kernel(width, source, up, down, block):
    blank = jnp.zeros((2, 16, HALF), f32)
    for x in range(NB):
        rows = slice(width * x, width * x + width)
        block[x, :, 0:16] = blank
        block[x, :, YE - 16:YE] = blank
        for h in range(2):
            up[h, rows] = source[x, NB - width:NB, lanes(h)].astype(f32)
            down[h, rows] = source[x, 0:width, lanes(h)].astype(f32)
            block[x, h, OFF:OFF + NB] = source[x, :, lanes(h)].astype(f32)


def join_rows(width, low, high, block):
    for x in range(NB):
        rows = slice(width * x, width * x + width)
        for h in range(2):
            block[x, h, OFF - width:OFF] = low[h, rows]
            block[x, h, OFF + NB:OFF + NB + width] = high[h, rows]


def join_label_kernel(low, high, _, block):
    join_rows(HL, low, high, block)


def join_field_kernel(low, high, label, _, __, block, up, down):
    join_rows(HB, low, high, block)
    for source, width in ((block, HB), (label, HL)):
        for d in range(1, width + 1):
            place, slab = sent_rows(d, source is label)
            for h in range(2):
                up[h, place] = source[NB - d, h, rows_of(slab)]
                down[h, place] = source[d - 1, h, rows_of(slab)]


def machine(arrays):
    west, east, south, north, below, above, diag, t, z, u = arrays

    def spread(ref, x, slab, finish):
        lane = lax.broadcasted_iota(jnp.int32, (slab[1] - slab[0], HALF), 1)
        at_low, at_high = lane == 0, lane == HALF - 1
        rows, real = rows_of(slab), held(slab)
        less, more = held((slab[0] - 1, slab[1] - 1)), held((slab[0] + 1, slab[1] + 1))
        here = tuple(ref[x, h, real] for h in range(2))
        back = tuple(pltpu.roll(here[h], 1, 1) for h in range(2))
        ahead = tuple(pltpu.roll(here[h], HALF - 1, 1) for h in range(2))
        lower = (back[0], jnp.where(at_low, back[0], back[1]))
        upper = (jnp.where(at_high, ahead[1], ahead[0]), ahead[1])
        for h in range(2):
            total = (
                (west[x, h, rows] * ref[x - 1, h, real] + east[x, h, rows] * ref[x + 1, h, real])
                + (south[x, h, rows] * ref[x, h, less] + north[x, h, rows] * ref[x, h, more])
                + (below[x, h, rows] * lower[h] + above[x, h, rows] * upper[h])
            )
            finish(h, here[h], total)

    def first(x, slab):
        def finish(h, here, total):
            z[x, h, held(slab)] = ZT * here + ZS * total
        spread(t, x, slab, finish)

    def second(x, slab):
        def finish(h, here, total):
            u[x, h, held(slab)] = UZ * here + UT * t[x, h, held(slab)] + US * total
        spread(z, x, slab, finish)

    def third(x, slab):
        def finish(h, here, total):
            t[x, h, held(slab)] = (t[x, h, held(slab)] - here) + total
        spread(u, x, slab, finish)

    steps = (first, second, third)

    def run(stage, start, stop):
        slab = FULL if stage < 4 else NEAR
        size = stop - start
        chunk = max(k for k in range(1, CHAIN + 1) if size % k == 0)
        if chunk < 5:
            chunk = CHAIN
        middle = stop - size % chunk

        def body(x, _):
            steps[stage % 3](x, slab)
            return 0
        lax.fori_loop(start, middle, body, 0, unroll=chunk)
        for x in range(middle, stop):
            steps[stage % 3](x, slab)

    def run_sides(stage):
        low, high = 2 + stage, HI - 2 - stage
        for slab, lo, hi in (((FULL if stage < 4 else NEAR), low + 5, high),
                             (NEAR, low, high + 5)):
            def body(i, _):
                steps[stage % 3](lo + i, slab)
                steps[stage % 3](hi + i, slab)
                return 0
            lax.fori_loop(0, 5, body, 0, unroll=5)

    def keep(ranges, u_out, r_out, pairs):
        own = slice(8 + OFF, 8 + OFF + NB)
        zero = jnp.zeros((NB, HALF), f32)

        def body(x, carry):
            totals = list(carry)
            for h in range(2):
                pre = u[x, h, own]
                res = t[x, h, own] * diag[x, h, OFF:OFF + NB]
                u_out[x - HL, :, lanes(h)] = pre
                r_out[x - HL, :, lanes(h)] = res
                for k, other in enumerate(pairs):
                    left = res if other is None else other[x - HL, :, lanes(h)]
                    totals[k] = totals[k] + left * pre
            return tuple(totals)

        totals = (zero,) * len(pairs)
        for start, stop in ranges:
            totals = lax.fori_loop(start, stop, body, totals)
        return totals

    return run, run_sides, keep


def kinds(table):
    def kind(labels):
        return jnp.where(labels == 1.0, 0.5 / table[1], jnp.where(
            labels == 2.0, 0.5 / table[2], jnp.where(
                labels == 3.0, 0.5 / table[3], 0.5 / table[0])))
    return kind


def coupler(table, arrays):
    west, east, south, north, below, above, diag, _, z, u = arrays
    lining = 0.5 / table[0]

    def row(x, labels, slab):
        lane = lax.broadcasted_iota(jnp.int32, (slab[1] - slab[0], HALF), 1)
        at_low, at_high = lane == 0, lane == HALF - 1
        rows, real = rows_of(slab), held(slab)
        less, more = held((slab[0] - 1, slab[1] - 1)), held((slab[0] + 1, slab[1] + 1))
        here = tuple(z[x, h, real] for h in range(2))
        after = tuple(pltpu.roll(here[h], HALF - 1, 1) for h in range(2))
        to_up = (1.0 / (here[0] + jnp.where(at_high, after[1], after[0])),
                 1.0 / (here[1] + jnp.where(at_high, lining, after[1])))
        moved = tuple(pltpu.roll(to_up[h], 1, 1) for h in range(2))
        to_down = (jnp.where(at_low, 1.0 / (here[0] + lining), moved[0]),
                   jnp.where(at_low, moved[0], moved[1]))
        for h in range(2):
            to_west = 1.0 / (here[h] + z[x - 1, h, real])
            to_east = 1.0 / (here[h] + z[x + 1, h, real])
            to_south = 1.0 / (here[h] + z[x, h, less])
            to_north = 1.0 / (here[h] + z[x, h, more])
            whole = to_west + to_east + to_south + to_north + to_down[h] + to_up[h]
            inverse = jnp.where(labels[h] > 0.0, 1.0 / whole, 0.0)
            west[x, h, rows] = to_west * inverse
            east[x, h, rows] = to_east * inverse
            south[x, h, rows] = to_south * inverse
            north[x, h, rows] = to_north * inverse
            down = to_down[h] * inverse
            rise = to_up[h] * inverse
            below[x, h, rows] = jnp.where(at_low, 0.0, down) if h == 0 else down
            above[x, h, rows] = jnp.where(at_high, 0.0, rise) if h == 1 else rise
            u[x, h, real] = inverse
            diag[x, h, rows] = whole

    return row


def as_line(parts):
    place = lax.broadcasted_iota(jnp.int32, (8, 128), 1)
    line = jnp.zeros((8, 128), f32)
    for k, part in enumerate(parts):
        line = jnp.where(place == k, jnp.sum(part), line)
    return line


LO, HI = HL, HL + NB
ROWS = 2 * HL


def own_kernel(table, label, *arrays):
    t, z, u = arrays[7:]
    kind = kinds(table)

    def clear(x, _):
        for ref in (t, z, u):
            ref[x, :, 0:8] = jnp.zeros((2, 8, HALF), f32)
            ref[x, :, 8 + YE:16 + YE] = jnp.zeros((2, 8, HALF), f32)
        return 0

    def clear_side(x, _):
        for side in (x, HI + x):
            for ref in (t, z, u):
                ref[side, :, 0:16] = jnp.zeros((2, 16, HALF), f32)
                ref[side, :, YE:16 + YE] = jnp.zeros((2, 16, HALF), f32)
        return 0
    lax.fori_loop(LO, HI, clear, 0, unroll=4)
    lax.fori_loop(0, HL, clear_side, 0, unroll=2)

    def translate(x, _):
        z[x + HL, :, 8:8 + YE] = kind(label[x])
        return 0
    lax.fori_loop(0, NB, translate, 0, unroll=2)
    row = coupler(table, arrays)

    def body(x, _):
        row(x, label[x - HL], FULL)
        return 0
    lax.fori_loop(LO + 1, HI - 1, body, 0, unroll=CU)


CU = 3
CHAIN = 8


def inner_kernel(rhs, field, *refs):
    arrays = refs[0:7] + refs[10:13]
    (r1, r2, r3, u0, u1, u2), sums = refs[13:19], refs[19]
    t, z, u = arrays[7:]
    run, _, keep = machine(arrays)

    def begin(x, _):
        t[x, :, 8:8 + YE] = field[x - HL] * u[x, :, 8:8 + YE]
        return 0
    lax.fori_loop(LO + 1, HI - 1, begin, 0, unroll=2)
    parts = ()
    for stage in range(9):
        rows = (LO + 2 + stage, HI - 2 - stage)
        run(stage, *rows)
        if stage == 2:
            parts += keep((rows,), u0, r1, (rhs, None))
        if stage == 5:
            parts += keep((rows,), u1, r2, (r1, None))
        if stage == 8:
            keep((rows,), u2, r3, ())
    sums[...] = as_line(parts)


def outer_kernel(table, rhs, label, field, low, high, part_sums, *refs):
    arrays = refs[16:26]
    (r1, r2, r3, u0, u1, u2), sums = refs[26:32], refs[32]
    t, z, u = arrays[7:]
    kind = kinds(table)
    row = coupler(table, arrays)
    for d in range(1, HL + 1):
        place, slab = sent_rows(d, True)
        for h in range(2):
            z[LO - d, h, held(slab)] = kind(low[h, place])
            z[HI - 1 + d, h, held(slab)] = kind(high[h, place])
    for x, k in ((LO, 0), (HI - 1, NB - 1)):
        row(x, label[k], FULL)
        t[x, :, held(FULL)] = field[k] * u[x, :, held(FULL)]

    def couple(d, slab, place, value):
        for x, source in ((LO - d, low), (HI - 1 + d, high)):
            row(x, tuple(source[h, place] for h in range(2)), slab)
            for h in range(2):
                t[x, h, held(slab)] = source[h, value] * u[x, h, held(slab)]

    for d in range(1, HB + 1):
        value, slab = sent_rows(d, False)
        place, whole = sent_rows(d, True)
        if whole != slab:
            place = slice(place.start + 8, place.stop - 8)
        couple(d, slab, place, value)
    _, run_sides, keep = machine(arrays)
    parts = ()
    for stage in range(9):
        run_sides(stage)
        rest = ((LO, LO + 2 + stage), (HI - 2 - stage, HI))
        if stage == 2:
            parts += keep(rest, u0, r1, (rhs, None))
        if stage == 5:
            parts += keep(rest, u1, r2, (r1, None))
        if stage == 8:
            keep(rest, u2, r3, ())
    sums[...] = part_sums[...] + as_line(parts)


CHUNK = 4


def final_kernel(sums, r0, r1, r2, r3, u0, u1, u2, solution_out, residual_out, pre_out,
                 image_out, bufs, sems):
    lane = lax.broadcasted_iota(jnp.int32, (8, 128), 1)
    total = sums[0:8, :]
    for k in range(1, 16):
        total = total + sums[8 * k:8 * k + 8, :]
    m0, m1, m2, m3 = (jnp.sum(jnp.where(lane == k, total, 0.0), axis=(0, 1), keepdims=True)
                      for k in range(4))
    curvature = m0 - m1
    step_one = m0 / curvature
    off_one = -m1 / curvature
    energy = off_one * off_one * m0 + 2.0 * off_one * step_one * m1 + step_one * step_one * m2
    bend = (off_one * off_one * (m0 - m1) + 2.0 * off_one * step_one * (m1 - m2)
            + step_one * step_one * (m2 - m3))
    momentum = energy / m0
    step_two = energy / (bend - momentum * energy / step_one)
    c2 = step_one * step_two
    c1 = step_one + step_two * (1.0 + momentum) - 2.0 * c2
    c0 = off_one * (1.0 - step_two) - step_two * momentum
    s0 = c1 + c2
    outs = (solution_out, residual_out, pre_out, image_out)
    copies = []
    for chunk in range(NB // CHUNK):
        def body(k, _):
            x = chunk * CHUNK + k
            v0, v1, v2, v3 = r0[x], r1[x], r2[x], r3[x]
            w0, w1, w2 = u0[x], u1[x], u2[x]
            bufs[0, x] = s0 * w0 + c2 * w1
            bufs[1, x] = c0 * v0 + c1 * v1 + c2 * v2
            bufs[2, x] = c0 * w0 + c1 * w1 + c2 * w2
            bufs[3, x] = c0 * (v0 - v1) + c1 * (v1 - v2) + c2 * (v2 - v3)
            return 0
        lax.fori_loop(0, CHUNK, body, 0)
        rows = slice(chunk * CHUNK, (chunk + 1) * CHUNK)
        for k in range(4):
            copy = pltpu.make_async_copy(bufs.at[k, rows], outs[k].at[rows], sems.at[chunk, k])
            copy.start()
            copies.append(copy)
    for copy in copies:
        copy.wait()


def neighbours(axis):
    count = lax.axis_size(axis)
    forward = [(i, i + 1) for i in range(count - 1)]
    return forward, [(target, source) for source, target in forward]


def swap(up, down, axis):
    forward, backward = neighbours(axis)
    return lax.ppermute(up, axis, forward), lax.ppermute(down, axis, backward)


def local(right_side, phase, table):
    def call(kernel, name, outs, ins, args, mib=2, cost=1, alias=(), scratch=()):
        return pl.pallas_call(
            kernel, name=name, in_specs=ins, out_specs=[VM] * len(outs), out_shape=outs,
            scratch_shapes=list(scratch), compiler_params=params(mib),
            input_output_aliases=dict(alias),
            cost_estimate=pl.CostEstimate(
                flops=0, bytes_accessed=int(cost * 2.5e6), transcendentals=0),
        )(*args)

    brick = shape(NB, NB, NZ)
    block = shape(NB, 2, YE, HALF)
    line = shape(8, 128)
    state = [shape(XE, 2, YE, HALF)] * 7 + [shape(XE, 2, YE + 16, HALF)] * 3

    def pack(source, width, name):
        return call(functools.partial(pack_kernel, width), name,
                    [shape(2, NB * width, HALF)] * 2 + [block], [VM], (source,))

    up_l, down_l, label = pack(phase, HL, "packlabel")
    up_f, down_f, field = pack(right_side, HB, "packfield")
    low_l, high_l = swap(up_l, down_l, "gy")
    low_f, high_f = swap(up_f, down_f, "gy")
    (label,) = call(join_label_kernel, "joinlabel", [block], [VM] * 3,
                    (low_l, high_l, label), alias={2: 0})
    arrays = call(own_kernel, "own", state, [SM, VM], (table, label), cost=5)
    field, up, down = call(
        join_field_kernel, "joinfield", [block] + [shape(2, SENT, HALF)] * 2,
        [VM] * 5, (low_f, high_f, label, arrays[9], field), alias={4: 0})
    low, high = swap(up, down, "gx")
    *mats, t, z, u = arrays
    *refs, sums = call(
        inner_kernel, "inner", state[7:] + [brick] * 6 + [line], [VM] * 12,
        (right_side, field, *mats, t, z, u), cost=10, alias={9 + k: k for k in range(3)})
    *refs, sums = call(
        outer_kernel, "outer", state + [brick] * 6 + [line], [SM] + [VM] * 22,
        (table, right_side, label, field, low, high, sums, *mats, *refs),
        cost=20, alias={7 + k: k for k in range(16)})
    r1, r2, r3, u0, u1, u2 = refs[10:]
    gathered = lax.all_to_all(
        jnp.broadcast_to(sums[0:1], (128, 128)), ("gx", "gy"), 0, 0, tiled=True)
    hbm = pl.BlockSpec(memory_space=pl.ANY)
    return pl.pallas_call(
        final_kernel, name="final", in_specs=[VM] * 8, out_specs=[hbm] * 4,
        out_shape=[brick] * 4,
        scratch_shapes=[pltpu.VMEM((4, NB, NB, NZ), f32),
                        pltpu.SemaphoreType.DMA((NB // CHUNK, 4))],
        compiler_params=params(6),
    )(gathered, right_side, r1, r2, r3, u0, u1, u2)


def solution(mesh):
    placed = (P("gx", "gy", None), P("gx", "gy", None), P())
    return jax.shard_map(
        local,
        mesh=mesh,
        in_specs=placed,
        out_specs=(P("gx", "gy", None),) * 4,
        check_vma=False,
    )
```

```python
import functools

import jax
import jax.numpy as jnp
from jax import lax
from jax.experimental import pallas as pl
from jax.experimental.pallas import tpu as pltpu
from jax.sharding import PartitionSpec as P

centre_value = 1.1
half_width = 0.9
ratio_sigma = centre_value / half_width
rho_first = 1.0 / ratio_sigma
rho_second = 1.0 / (2.0 * ratio_sigma - rho_first)
rho_third = 1.0 / (2.0 * ratio_sigma - rho_second)
start_scale = 1.0 / centre_value
keep_first = rho_second * rho_first
push_first = 2.0 * rho_second / half_width
keep_second = rho_third * rho_second
push_second = 2.0 * rho_third / half_width

ZT = (1.0 + keep_first - push_first) * start_scale + push_first
ZS = push_first * start_scale
UZ = 1.0 + keep_second - push_second
UT = push_second - keep_second * start_scale
US = push_second

NB = 32
HB = 9
HL = 10
OFF = 12
YE = 56
XE = NB + 2 * HL
NZ = 256
VM = pl.BlockSpec(memory_space=pltpu.VMEM)
SM = pl.BlockSpec(memory_space=pltpu.SMEM)
f32 = jnp.float32


def shape(*dims):
    return jax.ShapeDtypeStruct(dims, f32)


def params(mib):
    return pltpu.CompilerParams(vmem_limit_bytes=mib * 1024 * 1024)

HALF = NZ // 2
FULL, NEAR = (0, YE), (8, YE - 8)


def rows_of(slab):
    return slice(slab[0], slab[1])


def held(slab):
    return slice(slab[0] + 8, slab[1] + 8)


def sent_rows(distance, width):
    def size(d):
        return NB + 2 * (width - d)
    start = sum(size(d) for d in range(1, distance))
    if width == HL:
        start += sum(NB + 2 * (HB - d) for d in range(1, HB + 1))
    off = width - distance
    return slice(start, start + size(distance)), (OFF - off, OFF + NB + off)


SENT = -(-sent_rows(HL, HL)[0].stop // 8) * 8


def lanes(h):
    return slice(HALF * h, HALF * h + HALF)


def by_parity(axis, body, pair, other):
    odd = lax.rem(lax.axis_index(axis), 2)

    @pl.when(odd == 0)
    def _():
        body(pair, other)

    @pl.when(odd == 1)
    def _():
        body(other, pair)


def pack_kernel(width, source, pair, other, block):
    def send(up, down):
        for x in range(NB):
            rows = slice(width * x, width * x + width)
            for h in range(2):
                up[h, rows] = source[x, NB - width:NB, lanes(h)].astype(f32)
                down[h, rows] = source[x, 0:width, lanes(h)].astype(f32)
    by_parity("gy", send, pair, other)
    blank = jnp.zeros((2, 16, HALF), f32)
    for x in range(NB):
        block[x, :, 0:16] = blank
        block[x, :, YE - 16:YE] = blank
        for h in range(2):
            block[x, h, OFF:OFF + NB] = source[x, :, lanes(h)].astype(f32)


def join_rows(width, pair, other, block):
    def take(high, low):
        for x in range(NB):
            rows = slice(width * x, width * x + width)
            for h in range(2):
                block[x, h, OFF - width:OFF] = low[h, rows]
                block[x, h, OFF + NB:OFF + NB + width] = high[h, rows]
    by_parity("gy", take, pair, other)


def join_label_kernel(pair, other, _, block):
    join_rows(HL, pair, other, block)


def join_field_kernel(pair, other, label, _, __, block, pair_x, other_x):
    join_rows(HB, pair, other, block)

    def send(up, down):
        for source, width in ((block, HB), (label, HL)):
            for d in range(1, width + 1):
                place, slab = sent_rows(d, width)
                for h in range(2):
                    up[h, place] = source[NB - d, h, rows_of(slab)]
                    down[h, place] = source[d - 1, h, rows_of(slab)]
    by_parity("gx", send, pair_x, other_x)


def machine(arrays):
    west, east, south, north, below, above, diag, t, z, u = arrays

    def spread(ref, x, slab, finish):
        lane = lax.broadcasted_iota(jnp.int32, (slab[1] - slab[0], HALF), 1)
        at_low, at_high = lane == 0, lane == HALF - 1
        rows, real = rows_of(slab), held(slab)
        less, more = held((slab[0] - 1, slab[1] - 1)), held((slab[0] + 1, slab[1] + 1))
        here = tuple(ref[x, h, real] for h in range(2))
        back = tuple(pltpu.roll(here[h], 1, 1) for h in range(2))
        ahead = tuple(pltpu.roll(here[h], HALF - 1, 1) for h in range(2))
        lower = (back[0], jnp.where(at_low, back[0], back[1]))
        upper = (jnp.where(at_high, ahead[1], ahead[0]), ahead[1])
        for h in range(2):
            total = (
                (west[x, h, rows] * ref[x - 1, h, real] + east[x, h, rows] * ref[x + 1, h, real])
                + (south[x, h, rows] * ref[x, h, less] + north[x, h, rows] * ref[x, h, more])
                + (below[x, h, rows] * lower[h] + above[x, h, rows] * upper[h])
            )
            finish(h, here[h], total)

    def first(x, slab):
        def finish(h, here, total):
            z[x, h, held(slab)] = ZT * here + ZS * total
        spread(t, x, slab, finish)

    def second(x, slab):
        def finish(h, here, total):
            u[x, h, held(slab)] = UZ * here + UT * t[x, h, held(slab)] + US * total
        spread(z, x, slab, finish)

    def third(x, slab):
        def finish(h, here, total):
            t[x, h, held(slab)] = (t[x, h, held(slab)] - here) + total
        spread(u, x, slab, finish)

    steps = (first, second, third)

    def run(stage, start, stop):
        slab = FULL if stage < 4 else NEAR
        size = stop - start
        chunk = max(k for k in range(1, CHAIN + 1) if size % k == 0)
        if chunk < 5:
            chunk = CHAIN
        middle = stop - size % chunk

        def body(x, _):
            steps[stage % 3](x, slab)
            return 0
        lax.fori_loop(start, middle, body, 0, unroll=chunk)
        for x in range(middle, stop):
            steps[stage % 3](x, slab)

    def run_sides(stage):
        low, high = 2 + stage, HI - 2 - stage
        for slab, lo, hi in (((FULL if stage < 4 else NEAR), low + 5, high),
                             (NEAR, low, high + 5)):
            def body(i, _):
                steps[stage % 3](lo + i, slab)
                steps[stage % 3](hi + i, slab)
                return 0
            lax.fori_loop(0, 5, body, 0, unroll=5)

    def keep(ranges, u_out, r_out, pairs):
        own = slice(8 + OFF, 8 + OFF + NB)
        zero = jnp.zeros((NB, HALF), f32)

        def body(x, carry):
            totals = list(carry)
            for h in range(2):
                pre = u[x, h, own]
                res = t[x, h, own] * diag[x, h, OFF:OFF + NB]
                u_out[x - HL, :, lanes(h)] = pre
                r_out[x - HL, :, lanes(h)] = res
                for k, other in enumerate(pairs):
                    left = res if other is None else other[x - HL, :, lanes(h)]
                    totals[k] = totals[k] + left * pre
            return tuple(totals)

        totals = (zero,) * len(pairs)
        for start, stop in ranges:
            totals = lax.fori_loop(start, stop, body, totals)
        return totals

    return run, run_sides, keep


def kinds(table):
    def kind(labels):
        return jnp.where(labels == 1.0, 0.5 / table[1], jnp.where(
            labels == 2.0, 0.5 / table[2], jnp.where(
                labels == 3.0, 0.5 / table[3], 0.5 / table[0])))
    return kind


def coupler(table, arrays):
    west, east, south, north, below, above, diag, _, z, u = arrays
    lining = 0.5 / table[0]

    def row(x, marks, slab):
        lane = lax.broadcasted_iota(jnp.int32, (slab[1] - slab[0], HALF), 1)
        at_low, at_high = lane == 0, lane == HALF - 1
        rows, real = rows_of(slab), held(slab)
        less, more = held((slab[0] - 1, slab[1] - 1)), held((slab[0] + 1, slab[1] + 1))
        here = tuple(z[x, h, real] for h in range(2))
        after = tuple(pltpu.roll(here[h], HALF - 1, 1) for h in range(2))
        to_up = (1.0 / (here[0] + jnp.where(at_high, after[1], after[0])),
                 1.0 / (here[1] + jnp.where(at_high, lining, after[1])))
        moved = tuple(pltpu.roll(to_up[h], 1, 1) for h in range(2))
        to_down = (jnp.where(at_low, 1.0 / (here[0] + lining), moved[0]),
                   jnp.where(at_low, moved[0], moved[1]))
        for h in range(2):
            to_west = 1.0 / (here[h] + z[x - 1, h, real])
            to_east = 1.0 / (here[h] + z[x + 1, h, real])
            to_south = 1.0 / (here[h] + z[x, h, less])
            to_north = 1.0 / (here[h] + z[x, h, more])
            whole = to_west + to_east + to_south + to_north + to_down[h] + to_up[h]
            inverse = jnp.where(marks[h] > 0.0, 1.0 / whole, 0.0)
            west[x, h, rows] = to_west * inverse
            east[x, h, rows] = to_east * inverse
            south[x, h, rows] = to_south * inverse
            north[x, h, rows] = to_north * inverse
            down = to_down[h] * inverse
            rise = to_up[h] * inverse
            below[x, h, rows] = jnp.where(at_low, 0.0, down) if h == 0 else down
            above[x, h, rows] = jnp.where(at_high, 0.0, rise) if h == 1 else rise
            u[x, h, real] = inverse
            diag[x, h, rows] = whole

    return row


def as_line(parts):
    place = lax.broadcasted_iota(jnp.int32, (8, 128), 1)
    line = jnp.zeros((8, 128), f32)
    for k, part in enumerate(parts):
        line = jnp.where(place == k, jnp.sum(part), line)
    return line


LO, HI = HL, HL + NB
ROWS = 2 * HL


def own_kernel(table, label, *arrays):
    t, z, u = arrays[7:]
    kind = kinds(table)

    def clear(x, _):
        for ref in (t, z, u):
            ref[x, :, 0:8] = jnp.zeros((2, 8, HALF), f32)
            ref[x, :, 8 + YE:16 + YE] = jnp.zeros((2, 8, HALF), f32)
        return 0

    def clear_side(x, _):
        for side in (x, HI + x):
            t[side] = jnp.zeros((2, YE + 16, HALF), f32)
            z[side] = jnp.ones((2, YE + 16, HALF), f32)
            u[side] = jnp.zeros((2, YE + 16, HALF), f32)
        return 0
    lax.fori_loop(LO, HI, clear, 0, unroll=4)
    lax.fori_loop(0, HL, clear_side, 0, unroll=2)

    def translate(x, _):
        z[x + HL, :, 8:8 + YE] = kind(label[x])
        return 0
    lax.fori_loop(0, NB, translate, 0, unroll=2)
    row = coupler(table, arrays)

    def body(x, _):
        row(x, label[x - HL], FULL)
        return 0
    lax.fori_loop(LO + 1, HI - 1, body, 0, unroll=CU)


CU = 3
CHAIN = 14


def inner_kernel(rhs, field, *refs):
    arrays = refs[0:7] + refs[10:13]
    (r1, r2, r3, u0, u1, u2), sums = refs[13:19], refs[19]
    t, z, u = arrays[7:]
    run, _, keep = machine(arrays)

    def begin(x, _):
        t[x, :, 8:8 + YE] = field[x - HL] * u[x, :, 8:8 + YE]
        return 0
    lax.fori_loop(LO + 1, HI - 1, begin, 0, unroll=2)
    parts = ()
    for stage in range(9):
        rows = (LO + 2 + stage, HI - 2 - stage)
        run(stage, *rows)
        if stage == 2:
            parts += keep((rows,), u0, r1, (rhs, None))
        if stage == 5:
            parts += keep((rows,), u1, r2, (r1, None))
        if stage == 8:
            keep((rows,), u2, r3, ())
    sums[...] = as_line(parts)


def outer_kernel(table, rhs, label, field, pair, other, part_sums, *refs):
    arrays = refs[16:26]
    (r1, r2, r3, u0, u1, u2), sums = refs[26:32], refs[32]
    t, z, u = arrays[7:]
    kind = kinds(table)
    row = coupler(table, arrays)
    def take(high, low):
        for d in range(1, HL + 1):
            place, cells = sent_rows(d, HL)
            for x, source in ((LO - d, low), (HI - 1 + d, high)):
                for h in range(2):
                    z[x, h, held(cells)] = kind(source[h, place])
                    u[x, h, held(cells)] = source[h, place]
        for d in range(1, HB + 1):
            place, cells = sent_rows(d, HB)
            for x, source in ((LO - d, low), (HI - 1 + d, high)):
                for h in range(2):
                    t[x, h, held(cells)] = source[h, place]
    by_parity("gx", take, pair, other)
    for x, k in ((LO, 0), (HI - 1, NB - 1)):
        row(x, label[k], FULL)
        t[x, :, held(FULL)] = field[k] * u[x, :, held(FULL)]
    for d in range(1, HB + 1):
        slab = FULL if d < 5 else NEAR
        for x in (LO - d, HI - 1 + d):
            row(x, tuple(u[x, h, held(slab)] for h in range(2)), slab)
            t[x, :, held(slab)] = t[x, :, held(slab)] * u[x, :, held(slab)]
    _, run_sides, keep = machine(arrays)
    parts = ()
    for stage in range(9):
        run_sides(stage)
        rest = ((LO, LO + 2 + stage), (HI - 2 - stage, HI))
        if stage == 2:
            parts += keep(rest, u0, r1, (rhs, None))
        if stage == 5:
            parts += keep(rest, u1, r2, (r1, None))
        if stage == 8:
            keep(rest, u2, r3, ())
    sums[...] = part_sums[...] + as_line(parts)


CHUNK = 4


def final_kernel(sums, r0, r1, r2, r3, u0, u1, u2, solution_out, residual_out, pre_out,
                 image_out, bufs, sems):
    lane = lax.broadcasted_iota(jnp.int32, (8, 128), 1)
    total = sums[0:8, :]
    for k in range(1, 16):
        total = total + sums[8 * k:8 * k + 8, :]
    m0, m1, m2, m3 = (jnp.sum(jnp.where(lane == k, total, 0.0), axis=(0, 1), keepdims=True)
                      for k in range(4))
    curvature = m0 - m1
    step_one = m0 / curvature
    off_one = -m1 / curvature
    energy = off_one * off_one * m0 + 2.0 * off_one * step_one * m1 + step_one * step_one * m2
    bend = (off_one * off_one * (m0 - m1) + 2.0 * off_one * step_one * (m1 - m2)
            + step_one * step_one * (m2 - m3))
    momentum = energy / m0
    step_two = energy / (bend - momentum * energy / step_one)
    c2 = step_one * step_two
    c1 = step_one + step_two * (1.0 + momentum) - 2.0 * c2
    c0 = off_one * (1.0 - step_two) - step_two * momentum
    s0 = c1 + c2
    outs = (solution_out, residual_out, pre_out, image_out)
    copies = []
    for chunk in range(NB // CHUNK):
        def body(k, _):
            x = chunk * CHUNK + k
            v0, v1, v2, v3 = r0[x], r1[x], r2[x], r3[x]
            w0, w1, w2 = u0[x], u1[x], u2[x]
            bufs[0, x] = s0 * w0 + c2 * w1
            bufs[1, x] = c0 * v0 + c1 * v1 + c2 * v2
            bufs[2, x] = c0 * w0 + c1 * w1 + c2 * w2
            bufs[3, x] = c0 * (v0 - v1) + c1 * (v1 - v2) + c2 * (v2 - v3)
            return 0
        lax.fori_loop(0, CHUNK, body, 0)
        rows = slice(chunk * CHUNK, (chunk + 1) * CHUNK)
        for k in range(4):
            copy = pltpu.make_async_copy(bufs.at[k, rows], outs[k].at[rows], sems.at[chunk, k])
            copy.start()
            copies.append(copy)
    for copy in copies:
        copy.wait()


def exchange(pair, other, axis):
    count = lax.axis_size(axis)

    def swap(buffer, first):
        couples = [(i, i + 1) for i in range(first, count - 1, 2)]
        return lax.ppermute(buffer, axis, couples + [(b, a) for a, b in couples])
    return swap(pair, 0), swap(other, 1)


def local(right_side, phase, table):
    def call(kernel, name, outs, ins, args, mib=2, cost=1, alias=(), scratch=()):
        return pl.pallas_call(
            kernel, name=name, in_specs=ins, out_specs=[VM] * len(outs), out_shape=outs,
            scratch_shapes=list(scratch), compiler_params=params(mib),
            input_output_aliases=dict(alias),
            cost_estimate=pl.CostEstimate(
                flops=0, bytes_accessed=int(cost * 2.5e6), transcendentals=0),
        )(*args)

    brick = shape(NB, NB, NZ)
    block = shape(NB, 2, YE, HALF)
    line = shape(8, 128)
    state = [shape(XE, 2, YE, HALF)] * 7 + [shape(XE, 2, YE + 16, HALF)] * 3

    def pack(source, width, name):
        return call(functools.partial(pack_kernel, width), name,
                    [shape(2, NB * width, HALF)] * 2 + [block], [VM], (source,))

    *sent, label = pack(phase, HL, "packlabel")
    got_label = exchange(*sent, "gy")
    *sent, field = pack(right_side, HB, "packfield")
    got_field = exchange(*sent, "gy")
    (label,) = call(join_label_kernel, "joinlabel", [block], [VM] * 3,
                    (*got_label, label), alias={2: 0})
    arrays = call(own_kernel, "own", state, [SM, VM], (table, label), cost=5)
    field, *sent = call(
        join_field_kernel, "joinfield", [block] + [shape(2, SENT, HALF)] * 2,
        [VM] * 5, (*got_field, label, arrays[9], field), alias={4: 0})
    got = exchange(*sent, "gx")
    *mats, t, z, u = arrays
    *refs, sums = call(
        inner_kernel, "inner", state[7:] + [brick] * 6 + [line], [VM] * 12,
        (right_side, field, *mats, t, z, u), cost=10, alias={9 + k: k for k in range(3)})
    *refs, sums = call(
        outer_kernel, "outer", state + [brick] * 6 + [line], [SM] + [VM] * 22,
        (table, right_side, label, field, *got, sums, *mats, *refs),
        cost=20, alias={7 + k: k for k in range(16)})
    r1, r2, r3, u0, u1, u2 = refs[10:]
    gathered = lax.all_to_all(
        jnp.broadcast_to(sums[0:1], (128, 128)), ("gx", "gy"), 0, 0, tiled=True)
    hbm = pl.BlockSpec(memory_space=pl.ANY)
    return pl.pallas_call(
        final_kernel, name="final", in_specs=[VM] * 8, out_specs=[hbm] * 4,
        out_shape=[brick] * 4,
        scratch_shapes=[pltpu.VMEM((4, NB, NB, NZ), f32),
                        pltpu.SemaphoreType.DMA((NB // CHUNK, 4))],
        compiler_params=params(6),
    )(gathered, right_side, r1, r2, r3, u0, u1, u2)


def solution(mesh):
    placed = (P("gx", "gy", None), P("gx", "gy", None), P())
    return jax.shard_map(
        local,
        mesh=mesh,
        in_specs=placed,
        out_specs=(P("gx", "gy", None),) * 4,
        check_vma=False,
    )
```

```python
import functools

import jax
import jax.numpy as jnp
from jax import lax
from jax.experimental import pallas as pl
from jax.experimental.pallas import tpu as pltpu
from jax.sharding import PartitionSpec as P

centre_value = 1.1
half_width = 0.9
ratio_sigma = centre_value / half_width
rho_first = 1.0 / ratio_sigma
rho_second = 1.0 / (2.0 * ratio_sigma - rho_first)
rho_third = 1.0 / (2.0 * ratio_sigma - rho_second)
start_scale = 1.0 / centre_value
keep_first = rho_second * rho_first
push_first = 2.0 * rho_second / half_width
keep_second = rho_third * rho_second
push_second = 2.0 * rho_third / half_width

ZT = (1.0 + keep_first - push_first) * start_scale + push_first
ZS = push_first * start_scale
UZ = 1.0 + keep_second - push_second
UT = push_second - keep_second * start_scale
US = push_second

NB = 32
HB = 9
HL = 10
OFF = 12
YE = 56
XE = NB + 2 * HL
NZ = 256
VM = pl.BlockSpec(memory_space=pltpu.VMEM)
SM = pl.BlockSpec(memory_space=pltpu.SMEM)
f32 = jnp.float32


def shape(*dims):
    return jax.ShapeDtypeStruct(dims, f32)


def params(mib, flags=None):
    return pltpu.CompilerParams(vmem_limit_bytes=mib * 1024 * 1024, flags=flags)

HALF = NZ // 2
FULL, NEAR = (0, YE), (8, YE - 8)


def rows_of(slab):
    return slice(slab[0], slab[1])


def held(slab):
    return slice(slab[0] + 8, slab[1] + 8)


def sent_rows(distance, width):
    def size(d):
        return NB + 2 * (width - d)
    start = sum(size(d) for d in range(1, distance))
    if width == HL:
        start += sum(NB + 2 * (HB - d) for d in range(1, HB + 1))
    off = width - distance
    return slice(start, start + size(distance)), (OFF - off, OFF + NB + off)


SENT = -(-sent_rows(HL, HL)[0].stop // 8) * 8


def lanes(h):
    return slice(HALF * h, HALF * h + HALF)


def by_parity(axis, body, pair, other):
    odd = lax.rem(lax.axis_index(axis), 2)

    @pl.when(odd == 0)
    def _():
        body(pair, other)

    @pl.when(odd == 1)
    def _():
        body(other, pair)


def pack_kernel(width, source, pair, other, block):
    def send(up, down):
        for x in range(NB):
            rows = slice(width * x, width * x + width)
            for h in range(2):
                up[h, rows] = source[x, NB - width:NB, lanes(h)].astype(f32)
                down[h, rows] = source[x, 0:width, lanes(h)].astype(f32)
    by_parity("gy", send, pair, other)
    blank = jnp.zeros((2, 16, HALF), f32)
    for x in range(NB):
        block[x, :, 0:16] = blank
        block[x, :, YE - 16:YE] = blank
        for h in range(2):
            block[x, h, OFF:OFF + NB] = source[x, :, lanes(h)].astype(f32)


def join_rows(width, pair, other, block):
    def take(high, low):
        for x in range(NB):
            rows = slice(width * x, width * x + width)
            for h in range(2):
                block[x, h, OFF - width:OFF] = low[h, rows]
                block[x, h, OFF + NB:OFF + NB + width] = high[h, rows]
    by_parity("gy", take, pair, other)


def join_label_kernel(pair, other, _, block):
    join_rows(HL, pair, other, block)


def join_field_kernel(pair, other, label, _, __, block, pair_x, other_x):
    join_rows(HB, pair, other, block)

    def send(up, down):
        for source, width in ((block, HB), (label, HL)):
            for d in range(1, width + 1):
                place, slab = sent_rows(d, width)
                for h in range(2):
                    up[h, place] = source[NB - d, h, rows_of(slab)]
                    down[h, place] = source[d - 1, h, rows_of(slab)]
    by_parity("gx", send, pair_x, other_x)


def machine(arrays):
    west, east, south, north, below, above, diag, t, z, u = arrays

    def spread(ref, x, slab, finish):
        lane = lax.broadcasted_iota(jnp.int32, (slab[1] - slab[0], HALF), 1)
        at_low, at_high = lane == 0, lane == HALF - 1
        rows, real = rows_of(slab), held(slab)
        less, more = held((slab[0] - 1, slab[1] - 1)), held((slab[0] + 1, slab[1] + 1))
        here = tuple(ref[x, h, real] for h in range(2))
        back = tuple(pltpu.roll(here[h], 1, 1) for h in range(2))
        ahead = tuple(pltpu.roll(here[h], HALF - 1, 1) for h in range(2))
        lower = (back[0], jnp.where(at_low, back[0], back[1]))
        upper = (jnp.where(at_high, ahead[1], ahead[0]), ahead[1])
        for h in range(2):
            total = (
                (west[x, h, rows] * ref[x - 1, h, real] + east[x, h, rows] * ref[x + 1, h, real])
                + (south[x, h, rows] * ref[x, h, less] + north[x, h, rows] * ref[x, h, more])
                + (below[x, h, rows] * lower[h] + above[x, h, rows] * upper[h])
            )
            finish(h, here[h], total)

    def first(x, slab):
        def finish(h, here, total):
            z[x, h, held(slab)] = ZT * here + ZS * total
        spread(t, x, slab, finish)

    def second(x, slab):
        def finish(h, here, total):
            u[x, h, held(slab)] = UZ * here + UT * t[x, h, held(slab)] + US * total
        spread(z, x, slab, finish)

    def third(x, slab):
        def finish(h, here, total):
            t[x, h, held(slab)] = (t[x, h, held(slab)] - here) + total
        spread(u, x, slab, finish)

    steps = (first, second, third)

    def run(stage, start, stop):
        slab = FULL if stage < 4 else NEAR
        size = stop - start
        chunk = max(k for k in range(1, CHAIN + 1) if size % k == 0)
        if chunk < 5:
            chunk = CHAIN
        middle = stop - size % chunk

        def body(x, _):
            steps[stage % 3](x, slab)
            return 0
        lax.fori_loop(start, middle, body, 0, unroll=chunk)
        for x in range(middle, stop):
            steps[stage % 3](x, slab)

    def run_sides(stage):
        low, high = 2 + stage, HI - 2 - stage
        for slab, lo, hi in (((FULL if stage < 4 else NEAR), low + 5, high),
                             (NEAR, low, high + 5)):
            def body(i, _):
                steps[stage % 3](lo + i, slab)
                steps[stage % 3](hi + i, slab)
                return 0
            lax.fori_loop(0, 5, body, 0, unroll=5)

    def keep(ranges, u_out, r_out, pairs):
        own = slice(8 + OFF, 8 + OFF + NB)
        zero = jnp.zeros((NB, HALF), f32)

        def body(x, carry):
            totals = list(carry)
            for h in range(2):
                pre = u[x, h, own]
                res = t[x, h, own] * diag[x, h, OFF:OFF + NB]
                u_out[x - HL, :, lanes(h)] = pre
                r_out[x - HL, :, lanes(h)] = res
                for k, other in enumerate(pairs):
                    left = res if other is None else other[x - HL, :, lanes(h)]
                    totals[k] = totals[k] + left * pre
            return tuple(totals)

        totals = (zero,) * len(pairs)
        for start, stop in ranges:
            totals = lax.fori_loop(start, stop, body, totals, unroll=4)
        return totals

    return run, run_sides, keep


def kinds(table):
    def kind(labels):
        return jnp.where(labels == 1.0, 0.5 / table[1], jnp.where(
            labels == 2.0, 0.5 / table[2], jnp.where(
                labels == 3.0, 0.5 / table[3], 0.5 / table[0])))
    return kind


def coupler(table, arrays):
    west, east, south, north, below, above, diag, _, z, u = arrays
    lining = 0.5 / table[0]

    def row(x, marks, slab):
        lane = lax.broadcasted_iota(jnp.int32, (slab[1] - slab[0], HALF), 1)
        at_low, at_high = lane == 0, lane == HALF - 1
        rows, real = rows_of(slab), held(slab)
        less, more = held((slab[0] - 1, slab[1] - 1)), held((slab[0] + 1, slab[1] + 1))
        here = tuple(z[x, h, real] for h in range(2))
        after = tuple(pltpu.roll(here[h], HALF - 1, 1) for h in range(2))
        to_up = (1.0 / (here[0] + jnp.where(at_high, after[1], after[0])),
                 1.0 / (here[1] + jnp.where(at_high, lining, after[1])))
        moved = tuple(pltpu.roll(to_up[h], 1, 1) for h in range(2))
        to_down = (jnp.where(at_low, 1.0 / (here[0] + lining), moved[0]),
                   jnp.where(at_low, moved[0], moved[1]))
        for h in range(2):
            to_west = 1.0 / (here[h] + z[x - 1, h, real])
            to_east = 1.0 / (here[h] + z[x + 1, h, real])
            to_south = 1.0 / (here[h] + z[x, h, less])
            to_north = 1.0 / (here[h] + z[x, h, more])
            whole = to_west + to_east + to_south + to_north + to_down[h] + to_up[h]
            inverse = jnp.where(marks[h] > 0.0, 1.0 / whole, 0.0)
            west[x, h, rows] = to_west * inverse
            east[x, h, rows] = to_east * inverse
            south[x, h, rows] = to_south * inverse
            north[x, h, rows] = to_north * inverse
            down = to_down[h] * inverse
            rise = to_up[h] * inverse
            below[x, h, rows] = jnp.where(at_low, 0.0, down) if h == 0 else down
            above[x, h, rows] = jnp.where(at_high, 0.0, rise) if h == 1 else rise
            u[x, h, real] = inverse
            diag[x, h, rows] = whole

    return row


def as_line(parts):
    place = lax.broadcasted_iota(jnp.int32, (8, 128), 1)
    line = jnp.zeros((8, 128), f32)
    for k, part in enumerate(parts):
        short = (part[0:8] + part[8:16]) + (part[16:24] + part[24:32])
        line = jnp.where(place == k, jnp.sum(short, axis=(0, 1), keepdims=True), line)
    return line


LO, HI = HL, HL + NB
ROWS = 2 * HL


def own_kernel(table, label, *arrays):
    t, z, u = arrays[7:]
    kind = kinds(table)

    def clear(x, _):
        for ref in (t, z, u):
            ref[x, :, 0:8] = jnp.zeros((2, 8, HALF), f32)
            ref[x, :, 8 + YE:16 + YE] = jnp.zeros((2, 8, HALF), f32)
        return 0

    def clear_side(x, _):
        for side in (x, HI + x):
            t[side] = jnp.zeros((2, YE + 16, HALF), f32)
            z[side] = jnp.ones((2, YE + 16, HALF), f32)
            u[side] = jnp.zeros((2, YE + 16, HALF), f32)
        return 0
    lax.fori_loop(LO, HI, clear, 0, unroll=4)
    lax.fori_loop(0, HL, clear_side, 0, unroll=2)

    def translate(x, _):
        z[x + HL, :, 8:8 + YE] = kind(label[x])
        return 0
    lax.fori_loop(0, NB, translate, 0, unroll=2)
    row = coupler(table, arrays)

    def body(x, _):
        row(x, label[x - HL], FULL)
        return 0
    lax.fori_loop(LO + 1, HI - 1, body, 0, unroll=CU)


CU = 3
CHAIN = 14


def inner_kernel(rhs, field, *refs):
    arrays = refs[0:7] + refs[10:13]
    (r1, r2, r3, u0, u1, u2), sums = refs[13:19], refs[19]
    t, z, u = arrays[7:]
    run, _, keep = machine(arrays)

    def begin(x, _):
        t[x, :, 8:8 + YE] = field[x - HL] * u[x, :, 8:8 + YE]
        return 0
    lax.fori_loop(LO + 1, HI - 1, begin, 0, unroll=2)
    parts = ()
    for stage in range(9):
        rows = (LO + 2 + stage, HI - 2 - stage)
        run(stage, *rows)
        if stage == 2:
            parts += keep((rows,), u0, r1, (rhs, None))
        if stage == 5:
            parts += keep((rows,), u1, r2, (r1, None))
        if stage == 8:
            keep((rows,), u2, r3, ())
    for k, part in enumerate(parts):
        sums[k] = part


def outer_kernel(table, rhs, label, field, pair, other, part_sums, *refs):
    arrays = refs[16:26]
    (r1, r2, r3, u0, u1, u2), sums = refs[26:32], refs[32]
    t, z, u = arrays[7:]
    kind = kinds(table)
    row = coupler(table, arrays)
    def take(high, low):
        for d in range(1, HL + 1):
            place, cells = sent_rows(d, HL)
            for x, source in ((LO - d, low), (HI - 1 + d, high)):
                for h in range(2):
                    z[x, h, held(cells)] = kind(source[h, place])
                    u[x, h, held(cells)] = source[h, place]
        for d in range(1, HB + 1):
            place, cells = sent_rows(d, HB)
            for x, source in ((LO - d, low), (HI - 1 + d, high)):
                for h in range(2):
                    t[x, h, held(cells)] = source[h, place]
    by_parity("gx", take, pair, other)
    for x, k in ((LO, 0), (HI - 1, NB - 1)):
        row(x, label[k], FULL)
        t[x, :, held(FULL)] = field[k] * u[x, :, held(FULL)]
    for d in range(1, HB + 1):
        slab = FULL if d < 5 else NEAR
        for x in (LO - d, HI - 1 + d):
            row(x, tuple(u[x, h, held(slab)] for h in range(2)), slab)
            t[x, :, held(slab)] = t[x, :, held(slab)] * u[x, :, held(slab)]
    _, run_sides, keep = machine(arrays)
    parts = ()
    for stage in range(9):
        run_sides(stage)
        rest = ((LO, LO + 2 + stage), (HI - 2 - stage, HI))
        if stage == 2:
            parts += keep(rest, u0, r1, (rhs, None))
        if stage == 5:
            parts += keep(rest, u1, r2, (r1, None))
        if stage == 8:
            keep(rest, u2, r3, ())
    sums[...] = as_line([part + part_sums[k] for k, part in enumerate(parts)])


CHUNK = 4


def final_kernel(sums, r0, r1, r2, r3, u0, u1, u2, solution_out, residual_out, pre_out,
                 image_out, bufs, sems):
    lane = lax.broadcasted_iota(jnp.int32, (8, 128), 1)
    total = sums[0:8, :]
    for k in range(1, 16):
        total = total + sums[8 * k:8 * k + 8, :]
    m0, m1, m2, m3 = (jnp.sum(jnp.where(lane == k, total, 0.0), axis=(0, 1), keepdims=True)
                      for k in range(4))
    curvature = m0 - m1
    step_one = m0 / curvature
    off_one = -m1 / curvature
    energy = off_one * off_one * m0 + 2.0 * off_one * step_one * m1 + step_one * step_one * m2
    bend = (off_one * off_one * (m0 - m1) + 2.0 * off_one * step_one * (m1 - m2)
            + step_one * step_one * (m2 - m3))
    momentum = energy / m0
    step_two = energy / (bend - momentum * energy / step_one)
    c2 = step_one * step_two
    c1 = step_one + step_two * (1.0 + momentum) - 2.0 * c2
    c0 = off_one * (1.0 - step_two) - step_two * momentum
    s0 = c1 + c2
    outs = (solution_out, residual_out, pre_out, image_out)
    copies = []
    for chunk in range(NB // CHUNK):
        def body(k, _):
            x = chunk * CHUNK + k
            v0, v1, v2, v3 = r0[x], r1[x], r2[x], r3[x]
            w0, w1, w2 = u0[x], u1[x], u2[x]
            bufs[0, x] = s0 * w0 + c2 * w1
            bufs[1, x] = c0 * v0 + c1 * v1 + c2 * v2
            bufs[2, x] = c0 * w0 + c1 * w1 + c2 * w2
            bufs[3, x] = c0 * (v0 - v1) + c1 * (v1 - v2) + c2 * (v2 - v3)
            return 0
        lax.fori_loop(0, CHUNK, body, 0)
        rows = slice(chunk * CHUNK, (chunk + 1) * CHUNK)
        for k in range(4):
            copy = pltpu.make_async_copy(bufs.at[k, rows], outs[k].at[rows], sems.at[chunk, k])
            copy.start()
            copies.append(copy)
    for copy in copies:
        copy.wait()


def exchange(pair, other, axis):
    count = lax.axis_size(axis)

    def swap(buffer, first):
        couples = [(i, i + 1) for i in range(first, count - 1, 2)]
        return lax.ppermute(buffer, axis, couples + [(b, a) for a, b in couples])
    return swap(pair, 0), swap(other, 1)


def local(right_side, phase, table):
    def call(kernel, name, outs, ins, args, mib=2, cost=1, alias=(), scratch=(),
             flags=None):
        return pl.pallas_call(
            kernel, name=name, in_specs=ins, out_specs=[VM] * len(outs), out_shape=outs,
            scratch_shapes=list(scratch), compiler_params=params(mib, flags),
            input_output_aliases=dict(alias),
            cost_estimate=pl.CostEstimate(
                flops=0, bytes_accessed=int(cost * 2.5e6), transcendentals=0),
        )(*args)

    brick = shape(NB, NB, NZ)
    block = shape(NB, 2, YE, HALF)
    line = shape(8, 128)
    state = [shape(XE, 2, YE, HALF)] * 7 + [shape(XE, 2, YE + 16, HALF)] * 3

    def pack(source, width, name):
        return call(functools.partial(pack_kernel, width), name,
                    [shape(2, NB * width, HALF)] * 2 + [block], [VM], (source,))

    *sent, label = pack(phase, HL, "packlabel")
    got_label = exchange(*sent, "gy")
    *sent, field = pack(right_side, HB, "packfield")
    got_field = exchange(*sent, "gy")
    (label,) = call(join_label_kernel, "joinlabel", [block], [VM] * 3,
                    (*got_label, label), alias={2: 0})
    arrays = call(own_kernel, "own", state, [SM, VM], (table, label), cost=5)
    field, *sent = call(
        join_field_kernel, "joinfield", [block] + [shape(2, SENT, HALF)] * 2,
        [VM] * 5, (*got_field, label, arrays[9], field), alias={4: 0})
    got = exchange(*sent, "gx")
    *mats, t, z, u = arrays
    *refs, sums = call(
        inner_kernel, "inner", state[7:] + [brick] * 6 + [shape(4, NB, HALF)], [VM] * 12,
        (right_side, field, *mats, t, z, u), cost=10, alias={9 + k: k for k in range(3)})
    *refs, sums = call(
        outer_kernel, "outer", state + [brick] * 6 + [line], [SM] + [VM] * 22,
        (table, right_side, label, field, *got, sums, *mats, *refs),
        cost=20, alias={7 + k: k for k in range(16)})
    r1, r2, r3, u0, u1, u2 = refs[10:]
    gathered = lax.all_to_all(
        jnp.broadcast_to(sums[0:1], (128, 128)), ("gx", "gy"), 0, 0, tiled=True)
    hbm = pl.BlockSpec(memory_space=pl.ANY)
    return pl.pallas_call(
        final_kernel, name="final", in_specs=[VM] * 8, out_specs=[hbm] * 4,
        out_shape=[brick] * 4,
        scratch_shapes=[pltpu.VMEM((4, NB, NB, NZ), f32),
                        pltpu.SemaphoreType.DMA((NB // CHUNK, 4))],
        compiler_params=params(6),
    )(gathered, right_side, r1, r2, r3, u0, u1, u2)


def solution(mesh):
    placed = (P("gx", "gy", None), P("gx", "gy", None), P())
    return jax.shard_map(
        local,
        mesh=mesh,
        in_specs=placed,
        out_specs=(P("gx", "gy", None),) * 4,
        check_vma=False,
    )
```

```python
import functools

import jax
import jax.numpy as jnp
from jax import lax
from jax.experimental import pallas as pl
from jax.experimental.pallas import tpu as pltpu
from jax.sharding import PartitionSpec as P

centre_value = 1.1
half_width = 0.9
ratio_sigma = centre_value / half_width
rho_first = 1.0 / ratio_sigma
rho_second = 1.0 / (2.0 * ratio_sigma - rho_first)
rho_third = 1.0 / (2.0 * ratio_sigma - rho_second)
start_scale = 1.0 / centre_value
keep_first = rho_second * rho_first
push_first = 2.0 * rho_second / half_width
keep_second = rho_third * rho_second
push_second = 2.0 * rho_third / half_width

ZT = (1.0 + keep_first - push_first) * start_scale + push_first
ZS = push_first * start_scale
UZ = 1.0 + keep_second - push_second
UT = push_second - keep_second * start_scale
US = push_second

NB = 32
HB = 9
HL = 10
OFF = 12
YE = 56
XE = NB + 2 * HL
NZ = 256
VM = pl.BlockSpec(memory_space=pltpu.VMEM)
SM = pl.BlockSpec(memory_space=pltpu.SMEM)
f32 = jnp.float32


def shape(*dims):
    return jax.ShapeDtypeStruct(dims, f32)


def params(mib, flags=None):
    return pltpu.CompilerParams(vmem_limit_bytes=mib * 1024 * 1024, flags=flags)

HALF = NZ // 2
FULL, NEAR = (0, YE), (8, YE - 8)


def rows_of(slab):
    return slice(slab[0], slab[1])


def held(slab):
    return slice(slab[0] + 8, slab[1] + 8)


def sent_rows(distance, width):
    def size(d):
        return NB + 2 * (width - d)
    start = sum(size(d) for d in range(1, distance))
    if width == HL:
        start += sum(NB + 2 * (HB - d) for d in range(1, HB + 1))
    off = width - distance
    return slice(start, start + size(distance)), (OFF - off, OFF + NB + off)


SENT = -(-sent_rows(HL, HL)[0].stop // 8) * 8


def lanes(h):
    return slice(HALF * h, HALF * h + HALF)


def by_parity(axis, body, pair, other):
    odd = lax.rem(lax.axis_index(axis), 2)

    @pl.when(odd == 0)
    def _():
        body(pair, other)

    @pl.when(odd == 1)
    def _():
        body(other, pair)


def pack_kernel(width, source, pair, other, block):
    def send(up, down):
        for x in range(NB):
            rows = slice(width * x, width * x + width)
            for h in range(2):
                up[h, rows] = source[x, NB - width:NB, lanes(h)].astype(f32)
                down[h, rows] = source[x, 0:width, lanes(h)].astype(f32)
    by_parity("gy", send, pair, other)
    blank = jnp.zeros((2, 16, HALF), f32)
    for x in range(NB):
        block[x, :, 0:16] = blank
        block[x, :, YE - 16:YE] = blank
        for h in range(2):
            block[x, h, OFF:OFF + NB] = source[x, :, lanes(h)].astype(f32)


def join_rows(width, pair, other, block):
    def take(high, low):
        for x in range(NB):
            rows = slice(width * x, width * x + width)
            for h in range(2):
                block[x, h, OFF - width:OFF] = low[h, rows]
                block[x, h, OFF + NB:OFF + NB + width] = high[h, rows]
    by_parity("gy", take, pair, other)


def join_label_kernel(pair, other, _, block):
    join_rows(HL, pair, other, block)


def join_field_kernel(pair, other, label, _, __, block, pair_x, other_x):
    join_rows(HB, pair, other, block)

    def send(up, down):
        for source, width in ((block, HB), (label, HL)):
            for d in range(1, width + 1):
                place, slab = sent_rows(d, width)
                for h in range(2):
                    up[h, place] = source[NB - d, h, rows_of(slab)]
                    down[h, place] = source[d - 1, h, rows_of(slab)]
    by_parity("gx", send, pair_x, other_x)


def machine(arrays):
    west, east, south, north, below, above, diag, t, z, u = arrays

    def spread(ref, x, slab, finish):
        lane = lax.broadcasted_iota(jnp.int32, (slab[1] - slab[0], HALF), 1)
        at_low, at_high = lane == 0, lane == HALF - 1
        rows, real = rows_of(slab), held(slab)
        less, more = held((slab[0] - 1, slab[1] - 1)), held((slab[0] + 1, slab[1] + 1))
        here = tuple(ref[x, h, real] for h in range(2))
        back = tuple(pltpu.roll(here[h], 1, 1) for h in range(2))
        ahead = tuple(pltpu.roll(here[h], HALF - 1, 1) for h in range(2))
        lower = (back[0], jnp.where(at_low, back[0], back[1]))
        upper = (jnp.where(at_high, ahead[1], ahead[0]), ahead[1])
        for h in range(2):
            total = (
                (west[x, h, rows] * ref[x - 1, h, real] + east[x, h, rows] * ref[x + 1, h, real])
                + (south[x, h, rows] * ref[x, h, less] + north[x, h, rows] * ref[x, h, more])
                + (below[x, h, rows] * lower[h] + above[x, h, rows] * upper[h])
            )
            finish(h, here[h], total)

    def first(x, slab):
        def finish(h, here, total):
            z[x, h, held(slab)] = ZT * here + ZS * total
        spread(t, x, slab, finish)

    def second(x, slab):
        def finish(h, here, total):
            u[x, h, held(slab)] = UZ * here + UT * t[x, h, held(slab)] + US * total
        spread(z, x, slab, finish)

    def third(x, slab):
        def finish(h, here, total):
            t[x, h, held(slab)] = (t[x, h, held(slab)] - here) + total
        spread(u, x, slab, finish)

    steps = (first, second, third)

    def run(stage, start, stop):
        slab = FULL if stage < 4 else NEAR
        size = stop - start
        chunk = max(k for k in range(1, CHAIN + 1) if size % k == 0)
        if chunk < 5:
            chunk = CHAIN
        middle = stop - size % chunk

        def body(x, _):
            steps[stage % 3](x, slab)
            return 0
        lax.fori_loop(start, middle, body, 0, unroll=chunk)
        for x in range(middle, stop):
            steps[stage % 3](x, slab)

    def run_sides(stage):
        low, high = 2 + stage, HI - 2 - stage
        for slab, lo, hi in (((FULL if stage < 4 else NEAR), low + 5, high),
                             (NEAR, low, high + 5)):
            def body(i, _):
                steps[stage % 3](lo + i, slab)
                steps[stage % 3](hi + i, slab)
                return 0
            lax.fori_loop(0, 5, body, 0, unroll=5)

    def keep(ranges, u_out, r_out, pairs):
        own = slice(8 + OFF, 8 + OFF + NB)
        zero = jnp.zeros((NB, HALF), f32)

        def body(x, carry):
            totals = list(carry)
            for h in range(2):
                pre = u[x, h, own]
                res = t[x, h, own] * diag[x, h, OFF:OFF + NB]
                u_out[x - HL, :, lanes(h)] = pre
                r_out[x - HL, :, lanes(h)] = res
                for k, other in enumerate(pairs):
                    left = res if other is None else other[x - HL, :, lanes(h)]
                    totals[k] = totals[k] + left * pre
            return tuple(totals)

        totals = (zero,) * len(pairs)
        for start, stop in ranges:
            totals = lax.fori_loop(start, stop, body, totals, unroll=4)
        return totals

    return run, run_sides, keep


def kinds(table):
    def kind(labels):
        return jnp.where(labels == 1.0, 0.5 / table[1], jnp.where(
            labels == 2.0, 0.5 / table[2], jnp.where(
                labels == 3.0, 0.5 / table[3], 0.5 / table[0])))
    return kind


def coupler(table, arrays):
    west, east, south, north, below, above, diag, _, z, u = arrays
    lining = 0.5 / table[0]

    def row(x, marks, slab):
        lane = lax.broadcasted_iota(jnp.int32, (slab[1] - slab[0], HALF), 1)
        at_low, at_high = lane == 0, lane == HALF - 1
        rows, real = rows_of(slab), held(slab)
        less, more = held((slab[0] - 1, slab[1] - 1)), held((slab[0] + 1, slab[1] + 1))
        here = tuple(z[x, h, real] for h in range(2))
        after = tuple(pltpu.roll(here[h], HALF - 1, 1) for h in range(2))
        to_up = (1.0 / (here[0] + jnp.where(at_high, after[1], after[0])),
                 1.0 / (here[1] + jnp.where(at_high, lining, after[1])))
        moved = tuple(pltpu.roll(to_up[h], 1, 1) for h in range(2))
        to_down = (jnp.where(at_low, 1.0 / (here[0] + lining), moved[0]),
                   jnp.where(at_low, moved[0], moved[1]))
        for h in range(2):
            to_west = 1.0 / (here[h] + z[x - 1, h, real])
            to_east = 1.0 / (here[h] + z[x + 1, h, real])
            to_south = 1.0 / (here[h] + z[x, h, less])
            to_north = 1.0 / (here[h] + z[x, h, more])
            whole = to_west + to_east + to_south + to_north + to_down[h] + to_up[h]
            inverse = jnp.where(marks[h] > 0.0, 1.0 / whole, 0.0)
            west[x, h, rows] = to_west * inverse
            east[x, h, rows] = to_east * inverse
            south[x, h, rows] = to_south * inverse
            north[x, h, rows] = to_north * inverse
            down = to_down[h] * inverse
            rise = to_up[h] * inverse
            below[x, h, rows] = jnp.where(at_low, 0.0, down) if h == 0 else down
            above[x, h, rows] = jnp.where(at_high, 0.0, rise) if h == 1 else rise
            u[x, h, real] = inverse
            diag[x, h, rows] = whole

    return row


def as_line(parts):
    place = lax.broadcasted_iota(jnp.int32, (8, 128), 1)
    line = jnp.zeros((8, 128), f32)
    for k, part in enumerate(parts):
        short = (part[0:8] + part[8:16]) + (part[16:24] + part[24:32])
        line = jnp.where(place == k, jnp.sum(short, axis=(0, 1), keepdims=True), line)
    return line


LO, HI = HL, HL + NB
ROWS = 2 * HL


def own_kernel(table, label, *arrays):
    t, z, u = arrays[7:]
    kind = kinds(table)

    def clear(x, _):
        for ref in (t, z, u):
            ref[x, :, 0:8] = jnp.zeros((2, 8, HALF), f32)
            ref[x, :, 8 + YE:16 + YE] = jnp.zeros((2, 8, HALF), f32)
        return 0

    def clear_side(x, _):
        for side in (x, HI + x):
            t[side] = jnp.zeros((2, YE + 16, HALF), f32)
            z[side] = jnp.ones((2, YE + 16, HALF), f32)
            u[side] = jnp.zeros((2, YE + 16, HALF), f32)
        return 0
    lax.fori_loop(LO, HI, clear, 0, unroll=4)
    lax.fori_loop(0, HL, clear_side, 0, unroll=2)

    def translate(x, _):
        z[x + HL, :, 8:8 + YE] = kind(label[x])
        return 0
    lax.fori_loop(0, NB, translate, 0, unroll=2)
    row = coupler(table, arrays)

    def body(x, _):
        row(x, label[x - HL], FULL)
        return 0
    lax.fori_loop(LO + 1, HI - 1, body, 0, unroll=CU)


CU = 3
CHAIN = 14


def inner_kernel(rhs, field, *refs):
    arrays = refs[0:7] + refs[10:13]
    (r1, r2, r3, u0, u1, u2), sums = refs[13:19], refs[19]
    t, z, u = arrays[7:]
    run, _, keep = machine(arrays)

    def begin(x, _):
        t[x, :, 8:8 + YE] = field[x - HL] * u[x, :, 8:8 + YE]
        return 0
    lax.fori_loop(LO + 1, HI - 1, begin, 0, unroll=2)
    parts = ()
    for stage in range(9):
        rows = (LO + 2 + stage, HI - 2 - stage)
        run(stage, *rows)
        if stage == 2:
            parts += keep((rows,), u0, r1, (rhs, None))
        if stage == 5:
            parts += keep((rows,), u1, r2, (r1, None))
        if stage == 8:
            keep((rows,), u2, r3, ())
    for k, part in enumerate(parts):
        sums[k] = part


def outer_kernel(table, rhs, label, field, pair, other, part_sums, *refs):
    arrays = refs[16:26]
    (r1, r2, r3, u0, u1, u2), sums = refs[26:32], refs[32]
    t, z, u = arrays[7:]
    kind = kinds(table)
    row = coupler(table, arrays)
    def take(high, low):
        for d in range(1, HL + 1):
            place, cells = sent_rows(d, HL)
            for x, source in ((LO - d, low), (HI - 1 + d, high)):
                for h in range(2):
                    z[x, h, held(cells)] = kind(source[h, place])
                    u[x, h, held(cells)] = source[h, place]
        for d in range(1, HB + 1):
            place, cells = sent_rows(d, HB)
            for x, source in ((LO - d, low), (HI - 1 + d, high)):
                for h in range(2):
                    t[x, h, held(cells)] = source[h, place]
    by_parity("gx", take, pair, other)
    for x, k in ((LO, 0), (HI - 1, NB - 1)):
        row(x, label[k], FULL)
        t[x, :, held(FULL)] = field[k] * u[x, :, held(FULL)]
    for d in range(1, HB + 1):
        slab = FULL if d < 5 else NEAR
        for x in (LO - d, HI - 1 + d):
            row(x, tuple(u[x, h, held(slab)] for h in range(2)), slab)
            t[x, :, held(slab)] = t[x, :, held(slab)] * u[x, :, held(slab)]
    _, run_sides, keep = machine(arrays)
    parts = ()
    for stage in range(9):
        run_sides(stage)
        rest = ((LO, LO + 2 + stage), (HI - 2 - stage, HI))
        if stage == 2:
            parts += keep(rest, u0, r1, (rhs, None))
        if stage == 5:
            parts += keep(rest, u1, r2, (r1, None))
        if stage == 8:
            keep(rest, u2, r3, ())
    sums[...] = as_line([part + part_sums[k] for k, part in enumerate(parts)])


CHUNK = 2


def final_kernel(sums, r0, r1, r2, r3, u0, u1, u2, solution_out, residual_out, pre_out,
                 image_out, bufs, sems):
    lane = lax.broadcasted_iota(jnp.int32, (8, 128), 1)
    total = sums[0:8, :]
    for k in range(1, 16):
        total = total + sums[8 * k:8 * k + 8, :]
    m0, m1, m2, m3 = (jnp.sum(jnp.where(lane == k, total, 0.0), axis=(0, 1), keepdims=True)
                      for k in range(4))
    curvature = m0 - m1
    step_one = m0 / curvature
    off_one = -m1 / curvature
    energy = off_one * off_one * m0 + 2.0 * off_one * step_one * m1 + step_one * step_one * m2
    bend = (off_one * off_one * (m0 - m1) + 2.0 * off_one * step_one * (m1 - m2)
            + step_one * step_one * (m2 - m3))
    momentum = energy / m0
    step_two = energy / (bend - momentum * energy / step_one)
    c2 = step_one * step_two
    c1 = step_one + step_two * (1.0 + momentum) - 2.0 * c2
    c0 = off_one * (1.0 - step_two) - step_two * momentum
    s0 = c1 + c2
    outs = (solution_out, residual_out, pre_out, image_out)
    copies = []
    for chunk in range(NB // CHUNK):
        def body(k, _):
            x = chunk * CHUNK + k
            v0, v1, v2, v3 = r0[x], r1[x], r2[x], r3[x]
            w0, w1, w2 = u0[x], u1[x], u2[x]
            bufs[0, x] = s0 * w0 + c2 * w1
            bufs[1, x] = c0 * v0 + c1 * v1 + c2 * v2
            bufs[2, x] = c0 * w0 + c1 * w1 + c2 * w2
            bufs[3, x] = c0 * (v0 - v1) + c1 * (v1 - v2) + c2 * (v2 - v3)
            return 0
        lax.fori_loop(0, CHUNK, body, 0)
        rows = slice(chunk * CHUNK, (chunk + 1) * CHUNK)
        for k in range(4):
            copy = pltpu.make_async_copy(bufs.at[k, rows], outs[k].at[rows], sems.at[chunk, k])
            copy.start()
            copies.append(copy)
    for copy in copies:
        copy.wait()


def exchange(pair, other, axis):
    count = lax.axis_size(axis)

    def swap(buffer, first):
        couples = [(i, i + 1) for i in range(first, count - 1, 2)]
        return lax.ppermute(buffer, axis, couples + [(b, a) for a, b in couples])
    return swap(pair, 0), swap(other, 1)


def local(right_side, phase, table):
    def call(kernel, name, outs, ins, args, mib=2, cost=1, alias=(), scratch=(),
             flags=None):
        return pl.pallas_call(
            kernel, name=name, in_specs=ins, out_specs=[VM] * len(outs), out_shape=outs,
            scratch_shapes=list(scratch), compiler_params=params(mib, flags),
            input_output_aliases=dict(alias),
            cost_estimate=pl.CostEstimate(
                flops=0, bytes_accessed=int(cost * 2.5e6), transcendentals=0),
        )(*args)

    brick = shape(NB, NB, NZ)
    block = shape(NB, 2, YE, HALF)
    line = shape(8, 128)
    state = [shape(XE, 2, YE, HALF)] * 7 + [shape(XE, 2, YE + 16, HALF)] * 3

    def pack(source, width, name):
        return call(functools.partial(pack_kernel, width), name,
                    [shape(2, NB * width, HALF)] * 2 + [block], [VM], (source,))

    *sent, label = pack(phase, HL, "packlabel")
    got_label = exchange(*sent, "gy")
    *sent, field = pack(right_side, HB, "packfield")
    got_field = exchange(*sent, "gy")
    (label,) = call(join_label_kernel, "joinlabel", [block], [VM] * 3,
                    (*got_label, label), alias={2: 0})
    arrays = call(own_kernel, "own", state, [SM, VM], (table, label), cost=5)
    field, *sent = call(
        join_field_kernel, "joinfield", [block] + [shape(2, SENT, HALF)] * 2,
        [VM] * 5, (*got_field, label, arrays[9], field), alias={4: 0})
    got = exchange(*sent, "gx")
    *mats, t, z, u = arrays
    *refs, sums = call(
        inner_kernel, "inner", state[7:] + [brick] * 6 + [shape(4, NB, HALF)], [VM] * 12,
        (right_side, field, *mats, t, z, u), cost=10, alias={9 + k: k for k in range(3)})
    *refs, sums = call(
        outer_kernel, "outer", state + [brick] * 6 + [line], [SM] + [VM] * 22,
        (table, right_side, label, field, *got, sums, *mats, *refs),
        cost=20, alias={7 + k: k for k in range(16)})
    r1, r2, r3, u0, u1, u2 = refs[10:]
    gathered = lax.all_to_all(
        jnp.broadcast_to(sums[0:1], (128, 128)), ("gx", "gy"), 0, 0, tiled=True)
    hbm = pl.BlockSpec(memory_space=pl.ANY)
    return pl.pallas_call(
        final_kernel, name="final", in_specs=[VM] * 8, out_specs=[hbm] * 4,
        out_shape=[brick] * 4,
        scratch_shapes=[pltpu.VMEM((4, NB, NB, NZ), f32),
                        pltpu.SemaphoreType.DMA((NB // CHUNK, 4))],
        compiler_params=params(6),
    )(gathered, right_side, r1, r2, r3, u0, u1, u2)


def solution(mesh):
    placed = (P("gx", "gy", None), P("gx", "gy", None), P())
    return jax.shard_map(
        local,
        mesh=mesh,
        in_specs=placed,
        out_specs=(P("gx", "gy", None),) * 4,
        check_vma=False,
    )
```
